256 devices in a mesh: dp: 64 (over z_hi, x, y), ctx: 4 (over z_lo, core).
Axes of the slice: x: 4, y: 4, z: 8 (z_hi: 4, z_lo: 2; z = z_hi * 2 + z_lo), core: 2. Of those that a mesh axis runs over, the one named last changes fastest.
Arguments:
- latents: bfloat16 [32768, 2560], P(('dp', 'ctx')), may hold values from -6 to 6
- noise: bfloat16 [32768, 2560], P('dp', 'ctx'), may hold values from -6 to 6
- steps: int32 [64], replicated, may hold values from 0 to 999
- layout: int32 [64, 512], P('dp'), may hold values from 0 to 511, as said below
- w_time: bfloat16 [256, 7680], replicated, may hold values from -0.375 to 0.375
- w_student: bfloat16 [2560, 2560], P('dp', 'ctx'), may hold values from -0.125 to 0.125
- w_qk: bfloat16 [2560, 5120], P('dp', 'ctx'), may hold values from -4 to 4
- w_value: bfloat16 [2560, 2560], P('dp', 'ctx'), may hold values from -0.125 to 0.125
- w_disc: float32 [2560], P('ctx'), may hold values from -3 to 3
Outputs:
- clip_loss: float32 [64], replicated
- student_grad: float32 [2560, 2560], P('dp', 'ctx')
The draws below stay inside these ranges and needn't reach their ends.
Inputs may be any that keep to these rules, and one draw needn't show every extreme that they name: `layout`: each row holds every position of 0 to 511 once.
All inputs are finite; a program needn't handle non-finite values.
Results may differ from the reference program's by a relative error of at most 0.0059.
Values may be sent and summed in bfloat16 or wider, within the bound.
A program may use at most 128 MiB of HBM per device.

```python
import math
import jax
import jax.numpy as jnp
from jax import lax

D = 2560
HEADS = 20
HD = 128
FREQ = 256
STEPS = 1000
SEQ = 512
CLIPS = 64
TOKENS = 32768


def draw_w_qk(key, part):
    draws_base = jax.random.normal(key, (D, HEADS, 2, HD), jnp.float32) / jnp.sqrt(jnp.float32(D))
    return jnp.clip(draws_base, -4.0, 4.0).reshape(D, HEADS * 2 * HD).astype(jnp.bfloat16)


def clip_order(one_key):
    return jax.random.permutation(one_key, SEQ)


def draw_layout(key, part):
    clip_keys = jax.random.split(jax.random.fold_in(key, 41), CLIPS)
    orders = jax.vmap(clip_order)(clip_keys)
    return orders.astype(jnp.int32).reshape(CLIPS, SEQ)


def set_ends(drawn, key, smallest, top_value):
    longest = drawn.shape.index(max(drawn.shape))
    spots = []
    for shift in (0, 1):
        where = [jax.random.randint(jax.random.fold_in(key, axis), (), 0, length) for axis, length in enumerate(drawn.shape)]
        where[longest] = (where[longest] + shift) % drawn.shape[longest]
        spots.append(tuple(where))
    return drawn.at[spots[0]].set(smallest).at[spots[1]].set(top_value)


def block_levels(stream_key, dims, cuts, low, high):
    level, own = 1.0, jax.random.fold_in(stream_key, 6)
    for dim, shards_of in cuts:
        heights = jnp.exp(jax.random.uniform(jax.random.fold_in(own, dim), (shards_of,), jnp.float32, low / len(cuts), high / len(cuts)))
        level = level * jnp.repeat(heights, dims[dim] // shards_of).reshape([-1 if axis == dim else 1 for axis in range(len(dims))])
    return level


def normal_values(stream_key, dims, width, reach, cuts=(), kind=jnp.bfloat16):
    values = width * jax.random.normal(stream_key, dims, jnp.float32)
    if cuts:
        values = values * block_levels(stream_key, dims, cuts, -0.22, 0.18)
    return jnp.clip(values, -reach, reach).astype(kind)


def setup_inputs(seed: int = 0) -> dict:
    arg_keys = jax.random.split(jax.random.key(seed), 10)
    return {
        "latents": normal_values(arg_keys[0], (TOKENS, D), 1.0, 6.0, ((0, 256),)),
        "noise": normal_values(arg_keys[1], (TOKENS, D), 1.0, 6.0, ((0, 64), (1, 4))),
        "steps": set_ends(jax.random.randint(arg_keys[2], (CLIPS,), 0, STEPS), jax.random.fold_in(arg_keys[2], 1), 0, STEPS - 1).astype(jnp.int32),
        "layout": draw_layout(jax.random.fold_in(arg_keys[9], 71), 0),
        "w_time": normal_values(arg_keys[4], (FREQ, 3 * D), FREQ ** -0.5, 0.375),
        "w_student": normal_values(arg_keys[5], (D, D), D ** -0.5, 0.125, ((0, 64), (1, 4))),
        "w_qk": draw_w_qk(jax.random.fold_in(arg_keys[9], 71), 0),
        "w_value": normal_values(arg_keys[7], (D, D), D ** -0.5, 0.125, ((0, 64), (1, 4))),
        "w_disc": normal_values(arg_keys[8], (D,), 0.5, 3.0, ((0, 4),), jnp.float32),
    }


ln_eps = 1e-06
exact_dots = lax.Precision.HIGHEST

def normalize(matrix):
    mean_row = lax.optimization_barrier(jnp.mean(matrix, axis=-1, keepdims=True))
    centered = matrix - mean_row
    inverse = lax.rsqrt(lax.optimization_barrier(jnp.mean(centered * centered, axis=-1, keepdims=True)) + ln_eps)
    return (centered * inverse, inverse)

def time_embedding(steps):
    half_dim = FREQ // 2
    frequencies = jnp.exp(-math.log(10000.0) * jnp.arange(half_dim, dtype=jnp.float32) / half_dim)
    angles = steps.astype(jnp.float32)[:, None] * frequencies[None, :]
    return jnp.concatenate([jnp.cos(angles), jnp.sin(angles)], axis=1).astype(jnp.bfloat16)

def rotary_tables(positions):
    half_dim = HD // 2
    omegas = jnp.exp(-math.log(10000.0) * jnp.arange(half_dim, dtype=jnp.float32) / half_dim)
    angles = positions.astype(jnp.float32)[:, None] * omegas[None, :]
    return (jnp.cos(angles)[:, None, :], jnp.sin(angles)[:, None, :])

def rotate(values, cosine, sine_tab):
    half_dim = values.shape[-1] // 2
    first_half = values[..., :half_dim]
    second_half = values[..., half_dim:]
    return jnp.concatenate([first_half * cosine - second_half * sine_tab, first_half * sine_tab + second_half * cosine], axis=-1)

def unrotate(grads, cosine, sine_tab):
    half_dim = grads.shape[-1] // 2
    first_half = grads[..., :half_dim]
    second_half = grads[..., half_dim:]
    return jnp.concatenate([first_half * cosine + second_half * sine_tab, second_half * cosine - first_half * sine_tab], axis=-1)

def attend(query_group, key_f, head_values, seq_len):
    query_count = query_group.shape[0]
    block_len = min(query_count, 512)
    scale_dot = 1.0 / math.sqrt(HD)
    query_blocks = query_group.reshape(query_count // block_len, block_len, query_group.shape[1], HD)

    def block_step(state_in, query_block):
        d_keys, d_values, loss_sum = state_in
        query_f = query_block.astype(jnp.float32)
        scores = jnp.einsum('qhd,khd->hqk', query_f, key_f) * scale_dot
        row_top = lax.optimization_barrier(jnp.max(scores, axis=-1, keepdims=True))
        weights_exp = jnp.exp(scores - row_top)
        attn_probs = weights_exp / lax.optimization_barrier(jnp.sum(weights_exp, axis=-1, keepdims=True))
        logits = jnp.einsum('hqk,kh->q', attn_probs, head_values, precision=exact_dots)
        loss_sum = loss_sum + jnp.sum(jax.nn.softplus(-logits))
        d_logit = -jax.nn.sigmoid(-logits) / seq_len
        d_values = d_values + jnp.einsum('hqk,q->kh', attn_probs, d_logit, precision=exact_dots)
        d_probs = d_logit[None, :, None] * jnp.transpose(head_values)[:, None, :]
        row_delta = lax.optimization_barrier(jnp.sum(attn_probs * d_probs, axis=-1, keepdims=True))
        d_scores = (attn_probs * (d_probs - row_delta) * scale_dot).astype(jnp.bfloat16)
        d_scores_f = lax.optimization_barrier(d_scores).astype(jnp.float32)
        d_query = jnp.einsum('hqk,khd->qhd', d_scores_f, key_f)
        d_keys = d_keys + jnp.einsum('hqk,qhd->khd', d_scores_f, query_f)
        return ((d_keys, d_values, loss_sum), d_query)
    start_state = (jnp.zeros(key_f.shape, jnp.float32), jnp.zeros(head_values.shape, jnp.float32), jnp.zeros((), jnp.float32))
    (d_keys, d_values, loss_sum), d_query = lax.scan(block_step, start_state, query_blocks)
    return (d_query.reshape(query_group.shape), d_keys, d_values, loss_sum)

def clip_attention(query_rot, key_rot, values_b):
    seq_len = query_rot.shape[0]
    key_f = lax.optimization_barrier(key_rot).astype(jnp.float32)
    head_values = lax.optimization_barrier(values_b).astype(jnp.float32)
    query_all = lax.optimization_barrier(query_rot)
    d_query, d_keys, d_values, loss_sum = attend(query_all, key_f, head_values, seq_len)
    key_total = lax.optimization_barrier(d_keys.astype(jnp.bfloat16)).astype(jnp.float32)
    value_total = lax.optimization_barrier(d_values.astype(jnp.bfloat16)).astype(jnp.float32)
    return (d_query, key_total, value_total, loss_sum)

def clip_pass(latent_rows, noise_rows, modulation, sigma_clip, positions, w_student, w_qk, folded):
    seq_len, channels = latent_rows.shape
    head_count = folded.shape[1]
    shift_mod = modulation[:channels]
    scale_mod = modulation[channels:2 * channels]
    gate_mod = modulation[2 * channels:]
    normed, unused_inverse = normalize(latent_rows.astype(jnp.float32))
    mod_in = (normed * (1.0 + scale_mod) + shift_mod).astype(jnp.bfloat16)
    branch = jnp.dot(mod_in, w_student, preferred_element_type=jnp.float32)
    student_out = latent_rows.astype(jnp.float32) + gate_mod * branch
    teacher_in = ((1.0 - sigma_clip) * student_out + sigma_clip * noise_rows.astype(jnp.float32)).astype(jnp.bfloat16)
    tnorm, inverse = normalize(teacher_in.astype(jnp.float32))
    tnorm_b = tnorm.astype(jnp.bfloat16)
    qk_proj = jnp.dot(tnorm_b, w_qk, preferred_element_type=jnp.float32).reshape(seq_len, head_count, 2, HD)
    cosine, sine_tab = rotary_tables(positions)
    query_rot = rotate(qk_proj[:, :, 0], cosine, sine_tab).astype(jnp.bfloat16)
    key_rot = rotate(qk_proj[:, :, 1], cosine, sine_tab).astype(jnp.bfloat16)
    values_b = jnp.dot(tnorm_b, folded, precision=exact_dots, preferred_element_type=jnp.float32).astype(jnp.bfloat16)
    d_query, d_key, d_values, loss_sum = clip_attention(query_rot, key_rot, values_b)
    d_qk = jnp.stack([unrotate(d_query, cosine, sine_tab), unrotate(d_key, cosine, sine_tab)], axis=2)
    d_qk = d_qk.reshape(seq_len, head_count * 2 * HD).astype(jnp.bfloat16)
    d_tnorm = lax.dot_general(d_qk, w_qk, (((1,), (1,)), ((), ())), preferred_element_type=jnp.float32)
    d_tnorm = d_tnorm + lax.dot_general(d_values, folded, (((1,), (1,)), ((), ())), precision=exact_dots, preferred_element_type=jnp.float32)
    d_in = inverse * (d_tnorm - lax.optimization_barrier(jnp.mean(d_tnorm, axis=1, keepdims=True)) - tnorm * lax.optimization_barrier(jnp.mean(d_tnorm * tnorm, axis=1, keepdims=True)))
    d_branch = (gate_mod * (1.0 - sigma_clip) * d_in).astype(jnp.bfloat16)
    gradient = lax.dot_general(mod_in, d_branch, (((0,), (0,)), ((), ())), preferred_element_type=jnp.float32)
    return (loss_sum / seq_len, gradient)

def reference(latents, noise, steps, layout, w_time, w_student, w_qk, w_value, w_disc):
    channels = latents.shape[1]
    clip_count = steps.shape[0]
    seq_len = latents.shape[0] // clip_count
    modulation = jnp.dot(time_embedding(steps), w_time, preferred_element_type=jnp.float32)
    sigma_all = 0.25 + 0.5 * steps.astype(jnp.float32) / STEPS
    value_heads = w_value.astype(jnp.float32).reshape(channels, HEADS, HD)
    folded = jnp.einsum('rhd,hd->rh', value_heads, w_disc.reshape(HEADS, HD), precision=exact_dots)
    latent_clips = latents.reshape(clip_count, seq_len, channels)
    noise_clips = noise.reshape(clip_count, seq_len, channels)
    layout_clips = layout.reshape(clip_count, seq_len)

    def per_clip(running, inputs):
        latent_rows, noise_rows, mod_row, sigma_clip, positions = inputs
        loss_value, gradient = clip_pass(latent_rows, noise_rows, mod_row, sigma_clip, positions, w_student, w_qk, folded)
        return (running + gradient, loss_value)
    student_grad, clip_loss = lax.scan(per_clip, jnp.zeros((channels, channels), jnp.float32), (latent_clips, noise_clips, modulation, sigma_all, layout_clips))
    return (clip_loss, student_grad)
```

```python
import functools
import math

import jax
import jax.numpy as jnp
from jax import lax
from jax.experimental import pallas as pl
from jax.experimental.pallas import tpu as pltpu
from jax.sharding import PartitionSpec as P

HD = 128
FREQ = 256
STEPS = 1000
MESH = pl.DeviceIdType.MESH
VMEM = pltpu.VMEM
VSPEC = pl.BlockSpec(memory_space=pltpu.VMEM)
ASPEC = pl.BlockSpec(memory_space=pl.ANY)
F32 = jnp.float32
BF16 = jnp.bfloat16


ln_eps = 1e-06
exact_dots = lax.Precision.HIGHEST


def place():
    d = lax.axis_index("dp")
    c = lax.axis_index("ctx")
    return d // 16, (d // 4) % 4, d % 4, c // 2, c % 2


class Links:
    def __init__(self, send_sems, recv_sems):
        self.send_sems, self.recv_sems = send_sems, recv_sems
        self.used = 0
        self.open = []
        self.zh, self.x, self.y, self.zl, self.core = place()

    def dev(self, zh=0, x=0, y=0, zl=0, core=0):
        z_new = (self.zh + zh) % 4
        x_new = (self.x + x) % 4
        y_new = (self.y + y) % 4
        return (
            z_new * 16 + x_new * 4 + y_new,
            ((self.zl + zl) % 2) * 2 + (self.core + core) % 2,
        )

    def barrier(self, steps):
        sem = pltpu.get_barrier_semaphore()
        for step in steps:
            pl.semaphore_signal(sem, inc=1, device_id=self.dev(**step), device_id_type=MESH)
        pl.semaphore_wait(sem, len(steps))

    def send(self, src, dst, **step):
        slot = self.used
        self.used += 1
        copy = pltpu.make_async_remote_copy(
            src_ref=src,
            dst_ref=dst,
            send_sem=self.send_sems.at[slot],
            recv_sem=self.recv_sems.at[slot],
            device_id=self.dev(**step),
            device_id_type=MESH,
        )
        copy.start()
        self.open.append(copy)
        return copy

    def drain(self):
        for copy in self.open:
            copy.wait_send()


def comm_call(body, outs, ins, sems, cid, scratch, in_specs, out_specs):
    return pl.pallas_call(
        body,
        out_shape=outs,
        in_specs=in_specs,
        out_specs=out_specs,
        scratch_shapes=[
            pltpu.SemaphoreType.DMA((sems,)),
            pltpu.SemaphoreType.DMA((sems,)),
            *scratch,
        ],
        compiler_params=pltpu.CompilerParams(
            collective_id=cid, has_side_effects=True, vmem_limit_bytes=56 << 20
        ),
    )(*ins)


AXES_AB = (("x", "y", 0), ("y", "x", 2))


def slot_of(links, axis, step, other=None, zs=slice(0, 2)):
    moved = {"x": links.x, "y": links.y}
    moved[axis] = (moved[axis] + step) % 4
    picks = dict(moved)
    if other is not None:
        picks[other] = slice(None)
    return (zs, picks["x"], picks["y"])


class Gather:
    def __init__(self, links, shard, out, loc_sem):
        self.links, self.shard, self.out = links, shard, out
        self.own = pltpu.make_async_copy(shard, out.at[links.zh, links.x, links.y], loc_sem)

    def along_z(self):
        links = self.links
        self.own.start()
        home = self.out.at[links.zh, links.x, links.y]
        self.copies = [links.send(self.shard, home, zh=step) for step in (1, 3, 2)]

    def settle(self):
        for copy in self.copies:
            copy.wait_recv()
        self.copies = []

    def spread(self, second):
        links = self.links
        if not second:
            self.own.wait()
        self.settle()
        self.near = []
        for first_axis, second_axis, base in AXES_AB:
            axis = second_axis if second else first_axis
            other = first_axis if second else None
            mine = self.out.at[slot_of(links, axis, 0, other, slice(base, base + 2))]
            self.near.append(
                (
                    axis,
                    other,
                    base,
                    links.send(mine, mine, **{axis: 1}),
                    links.send(mine, mine, **{axis: 3}),
                )
            )

    def relay(self):
        links = self.links
        self.copies = []
        for axis, other, base, up, down in self.near:
            up.wait_recv()
            piece = self.out.at[slot_of(links, axis, 3, other, base)]
            self.copies.append(links.send(piece, piece, **{axis: 1}))
            down.wait_recv()
            piece = self.out.at[slot_of(links, axis, 1, other, base + 1)]
            self.copies.append(links.send(piece, piece, **{axis: 3}))


NEAR = (
    dict(zh=1),
    dict(zh=2),
    dict(zh=3),
    dict(x=1),
    dict(x=3),
    dict(y=1),
    dict(y=3),
)


def gather_body(
    ws, wqk, fold, lat, ws_o, wqk_o, fold_o, lat_o, send_sems, recv_sems, loc_sems
):
    links = Links(send_sems, recv_sems)
    links.barrier(NEAR + (dict(core=1), dict(zl=1)))
    me = links.zl * 2 + links.core
    far = ((links.zl + 1) % 2) * 2 + links.core
    g_ws = Gather(links, ws, ws_o, loc_sems.at[0])
    g_fold = Gather(links, fold, fold_o, loc_sems.at[1])
    g_wqk = Gather(links, wqk, wqk_o, loc_sems.at[2])
    early = (g_ws, g_fold)
    for gather in early + (g_wqk,):
        gather.along_z()
    own = pltpu.make_async_copy(lat, lat_o.at[me], loc_sems.at[3])
    own.start()
    halves = [slice(0, 64), slice(64, 128)]
    across = [links.send(lat.at[h], lat_o.at[me, h], zl=1) for h in halves]
    beside = links.send(lat, lat_o.at[me], core=1)
    for gather in early + (g_wqk,):
        gather.spread(False)
    for gather in early:
        gather.relay()
    for gather in early:
        gather.spread(True)
    g_wqk.relay()
    for gather in early:
        gather.relay()
    g_wqk.spread(True)
    passed = []
    for copy, h in zip(across, halves):
        copy.wait_recv()
        passed.append(links.send(lat_o.at[far, h], lat_o.at[far, h], core=1))
    for gather in early:
        gather.settle()
    g_wqk.relay()
    own.wait()
    beside.wait_recv()
    for copy in passed:
        copy.wait_recv()
    g_wqk.settle()
    links.drain()


def gather_all(ws, wqk, fold, lat):
    outs = (
        jax.ShapeDtypeStruct((4, 4, 4) + ws.shape, ws.dtype),
        jax.ShapeDtypeStruct((4, 4, 4) + wqk.shape, wqk.dtype),
        jax.ShapeDtypeStruct((4, 4, 4) + fold.shape, fold.dtype),
        jax.ShapeDtypeStruct((4,) + lat.shape, lat.dtype),
    )
    return comm_call(
        gather_body,
        outs,
        (ws, wqk, fold, lat),
        64,
        1,
        [pltpu.SemaphoreType.DMA((4,))],
        [VSPEC] * 4,
        [ASPEC] * 4,
    )


CLIP_NEAR = (dict(core=1), dict(zl=1))
CLIP_ALL = CLIP_NEAR + (dict(zl=1, core=1),)


def teacher_body(part, full, send_sems, recv_sems, loc_sem):
    links = Links(send_sems, recv_sems)
    rows, cols = part.shape
    chunk = rows // 4

    def cut(owner, index):
        start = pl.multiple_of(owner * cols, 128)
        return full.at[pl.ds(index * chunk, chunk), pl.ds(start, cols)]

    me = links.zl * 2 + links.core
    far = ((links.zl + 1) % 2) * 2 + links.core
    links.barrier(CLIP_NEAR)
    own = pltpu.make_async_copy(part, full.at[:, pl.ds(pl.multiple_of(me * cols, 128), cols)], loc_sem)
    own.start()
    across, beside = [], []
    for index in range(4):
        piece = part.at[pl.ds(index * chunk, chunk)]
        across.append(links.send(piece, cut(me, index), zl=1))
        beside.append(links.send(piece, cut(me, index), core=1))
    passed = []
    for index, copy in enumerate(across):
        copy.wait_recv()
        passed.append(links.send(cut(far, index), cut(far, index), core=1))
    for copy in beside + passed:
        copy.wait_recv()
    own.wait()
    links.drain()


def teacher_gather(part):
    rows, cols = part.shape
    return comm_call(
        teacher_body,
        jax.ShapeDtypeStruct((rows, 4 * cols), part.dtype),
        (part,),
        12,
        2,
        [pltpu.SemaphoreType.DMA],
        [VSPEC],
        VSPEC,
    )


def reduce_clip_body(
    part, stats, out, stats_o, send_sems, recv_sems, stage, from_core, cross, from_chip, stats_in
):
    links = Links(send_sems, recv_sems)
    rows, cols = out.shape
    chunk = rows // 4
    core, zl = links.core, links.zl
    links.barrier(CLIP_ALL)
    tiny = [
        links.send(stats, stats_in.at[index], **step) for index, step in enumerate(CLIP_ALL)
    ]

    def block(z_to, core_to, index):
        start = pl.multiple_of((z_to * 2 + core_to) * cols, 128)
        return part[pl.ds(index * chunk, chunk), pl.ds(start, cols)]

    first = []
    for side in (1, 0):
        z_to = (zl + side) % 2
        for index in range(4):
            here = (side, pl.ds(index * chunk, chunk))
            stage[here] = block(z_to, (core + 1) % 2, index).astype(BF16)
            first.append(links.send(stage.at[here], from_core.at[here], core=1))
    second = []
    for index in range(4):
        here = (1, pl.ds(index * chunk, chunk))
        first[index].wait_recv()
        total = block((zl + 1) % 2, core, index) + from_core[here].astype(F32)
        rows_here = pl.ds(index * chunk, chunk)
        cross[rows_here] = total.astype(BF16)
        second.append(links.send(cross.at[rows_here], from_chip.at[rows_here], zl=1))
    for index in range(4):
        rows_here = pl.ds(index * chunk, chunk)
        first[4 + index].wait_recv()
        out[rows_here] = block(zl, core, index) + from_core[0, rows_here].astype(F32)
    for copy in tiny:
        copy.wait_recv()
    stats_o[...] = stats[...] + stats_in[0] + stats_in[1] + stats_in[2]
    for index in range(4):
        rows_here = pl.ds(index * chunk, chunk)
        second[index].wait_recv()
        out[rows_here] = out[rows_here] + from_chip[rows_here].astype(F32)
    links.drain()


def reduce_clip(part, stats):
    rows, cols = part.shape[0], part.shape[1] // 4
    return comm_call(
        reduce_clip_body,
        (
            jax.ShapeDtypeStruct((rows, cols), F32),
            jax.ShapeDtypeStruct(stats.shape, F32),
        ),
        (part, stats),
        15,
        3,
        [
            VMEM((2, rows, cols), BF16),
            VMEM((2, rows, cols), BF16),
            VMEM((rows, cols), BF16),
            VMEM((rows, cols), BF16),
            VMEM((3,) + stats.shape, F32),
        ],
        [VSPEC, VSPEC],
        (VSPEC, VSPEC),
    )


class Scatter:
    def __init__(self, links, axis, read, plain, bufs):
        self.links, self.axis, self.read, self.plain = links, axis, read, plain
        self.one_up, self.one_down, self.mix_up, self.mix_down, self.two_up, self.two_down = bufs

    def start(self):
        links, axis, plain = self.links, self.axis, self.plain
        self.up = links.send(plain(0, 2), self.one_up, **{axis: 1})
        self.down = links.send(plain(1, 2), self.one_down, **{axis: 3})
        self.last = [
            links.send(plain(1, 1), self.two_up.at[1], **{axis: 1}),
            links.send(plain(0, 3), self.two_down.at[0], **{axis: 3}),
        ]

    def middle(self):
        links, axis = self.links, self.axis
        self.up.wait_recv()
        self.mix_up[...] = (self.read(0, 1) + self.one_up[...].astype(F32)).astype(BF16)
        self.last.append(links.send(self.mix_up, self.two_up.at[0], **{axis: 1}))
        self.down.wait_recv()
        self.mix_down[...] = (self.read(1, 3) + self.one_down[...].astype(F32)).astype(BF16)
        self.last.append(links.send(self.mix_down, self.two_down.at[1], **{axis: 3}))

    def finish(self, store):
        for copy in self.last:
            copy.wait_recv()
        for half in range(2):
            store(
                half,
                self.read(half, 0)
                + self.two_up[half].astype(F32)
                + self.two_down[half].astype(F32),
            )


SCATTER_NEAR = NEAR + (dict(x=2), dict(y=2))


def scatter_body(part, loss, out, loss_o, send_sems, recv_sems, loss_buf, loss_mid, z_send, z_recv, z_keep, *bufs):
    links = Links(send_sems, recv_sems)
    links.barrier(SCATTER_NEAR)
    spare = list(bufs)
    stages = []
    for first_axis, second_axis, base in (("y", "x", 0), ("x", "y", 2)):
        big, spare = spare[:6], spare[6:]
        small, spare = spare[:6], spare[6:]
        mid, mid_b, spare = spare[0], spare[1], spare[2:]

        def plain1(half, step, axis=first_axis, other=second_axis, base=base):
            return part.at[slot_of(links, axis, step, other, base + half)]

        def read1(half, step, plain=plain1):
            return plain(half, step)[...].astype(F32)

        def spot(step, axis=second_axis):
            return ({"x": links.x, "y": links.y}[axis] + step) % 4

        def plain2(half, step, mid_b=mid_b, spot=spot):
            return mid_b.at[half, spot(step)]

        def read2(half, step, mid=mid, spot=spot):
            return mid[half, spot(step)]

        stages.append(
            (
                base,
                mid,
                mid_b,
                Scatter(links, first_axis, read1, plain1, big),
                Scatter(links, second_axis, read2, plain2, small),
            )
        )
    loss_mid[0] = loss[...]
    for stage in stages:
        stage[3].start()

    def loss_step(index, axis):
        return [
            links.send(loss_mid.at[index], loss_buf.at[index, step - 1], **{axis: step})
            for step in (1, 2, 3)
        ]

    def loss_sum(index, copies, store):
        for copy in copies:
            copy.wait_recv()
        store(loss_mid[index] + loss_buf[index, 0] + loss_buf[index, 1] + loss_buf[index, 2])

    def put_mid(index, value):
        loss_mid[index] = value

    tiny = loss_step(0, "y")
    for stage in stages:
        stage[3].middle()
    loss_sum(0, tiny, functools.partial(put_mid, 1))
    tiny = loss_step(1, "x")
    for base, mid, mid_b, first, second in stages:

        def store(half, value, mid=mid, mid_b=mid_b):
            mid[half] = value
            mid_b[half] = value.astype(BF16)

        first.finish(store)
        second.start()
    loss_sum(1, tiny, functools.partial(put_mid, 2))
    tiny = loss_step(2, "zh")
    for stage in stages:
        stage[4].middle()
    for base, mid, mid_b, first, second in stages:

        def keep(half, value, base=base):
            z_keep[base + half] = value
            z_send[base + half] = value.astype(BF16)

        second.finish(keep)
    tail = [
        links.send(z_send.at[(links.zh + step) % 4], z_recv.at[step - 1], zh=step)
        for step in (1, 3, 2)
    ]

    def put_loss(value):
        loss_o[...] = value

    loss_sum(2, tiny, put_loss)
    for copy in tail:
        copy.wait_recv()
    out[...] = (
        z_keep[links.zh]
        + z_recv[0].astype(F32)
        + z_recv[1].astype(F32)
        + z_recv[2].astype(F32)
    )
    links.drain()


def scatter_all(part, loss):
    rows, cols = part.shape[3:]
    big = [VMEM((4, rows, cols), BF16)] * 4 + [VMEM((2, 4, rows, cols), BF16)] * 2
    small = [VMEM((rows, cols), BF16)] * 4 + [VMEM((2, rows, cols), BF16)] * 2
    mids = [VMEM((2, 4, rows, cols), F32), VMEM((2, 4, rows, cols), BF16)]
    return comm_call(
        scatter_body,
        (
            jax.ShapeDtypeStruct((rows, cols), F32),
            jax.ShapeDtypeStruct(loss.shape, F32),
        ),
        (part, loss),
        40,
        4,
        [
            VMEM((3, 3) + loss.shape, F32),
            VMEM((3,) + loss.shape, F32),
            VMEM((4, rows, cols), BF16),
            VMEM((3, rows, cols), BF16),
            VMEM((4, rows, cols), F32),
        ]
        + (big + small + mids) * 2,
        [VSPEC, VSPEC],
        (VSPEC, VSPEC),
    )


def normalize(matrix):
    mean_row = jnp.mean(matrix, axis=-1, keepdims=True)
    centered = matrix - mean_row
    inverse = lax.rsqrt(jnp.mean(centered * centered, axis=-1, keepdims=True) + ln_eps)
    return (centered * inverse, inverse)


def time_embedding(steps):
    half_dim = FREQ // 2
    frequencies = jnp.exp(-math.log(10000.0) * jnp.arange(half_dim, dtype=jnp.float32) / half_dim)
    angles = steps.astype(jnp.float32)[:, None] * frequencies[None, :]
    return jnp.concatenate([jnp.cos(angles), jnp.sin(angles)], axis=1).astype(jnp.bfloat16)


def rotary_tables(positions):
    half_dim = HD // 2
    omegas = jnp.exp(-math.log(10000.0) * jnp.arange(half_dim, dtype=jnp.float32) / half_dim)
    angles = positions.astype(jnp.float32)[:, None] * omegas[None, :]
    return (jnp.cos(angles)[:, None, :], jnp.sin(angles)[:, None, :])


def rotate(values, cosine, sine_tab):
    half_dim = values.shape[-1] // 2
    first_half = values[..., :half_dim]
    second_half = values[..., half_dim:]
    return jnp.concatenate(
        [
            first_half * cosine - second_half * sine_tab,
            first_half * sine_tab + second_half * cosine,
        ],
        axis=-1,
    )


def unrotate(grads, cosine, sine_tab):
    half_dim = grads.shape[-1] // 2
    first_half = grads[..., :half_dim]
    second_half = grads[..., half_dim:]
    return jnp.concatenate(
        [
            first_half * cosine + second_half * sine_tab,
            second_half * cosine - first_half * sine_tab,
        ],
        axis=-1,
    )


def attend(query_block, key_all, value_all, seq_len):
    scale_dot = 1.0 / math.sqrt(HD)
    head_values = value_all.astype(jnp.float32)
    values_by_head = jnp.transpose(head_values)
    scores = (
        jnp.einsum("qhd,khd->hqk", query_block, key_all, preferred_element_type=jnp.float32)
        * scale_dot
    )
    row_top = jnp.max(scores, axis=-1, keepdims=True)
    weights_exp = jnp.exp(scores - row_top)
    attn_probs = weights_exp / jnp.sum(weights_exp, axis=-1, keepdims=True)
    partial_value = jnp.einsum("hqk,kh->q", attn_probs, head_values, precision=exact_dots)
    logits = lax.psum(partial_value, "ctx")
    loss_sum = jnp.sum(jax.nn.softplus(-logits))
    d_logit = -jax.nn.sigmoid(-logits) / seq_len
    d_values = jnp.einsum("hqk,q->kh", attn_probs, d_logit, precision=exact_dots)
    d_probs = d_logit[None, :, None] * values_by_head[:, None, :]
    row_delta = jnp.sum(attn_probs * d_probs, axis=-1, keepdims=True)
    d_scores = (attn_probs * (d_probs - row_delta) * scale_dot).astype(jnp.bfloat16)
    d_query = jnp.einsum("hqk,khd->qhd", d_scores, key_all, preferred_element_type=jnp.float32)
    d_keys = jnp.einsum("hqk,qhd->khd", d_scores, query_block, preferred_element_type=jnp.float32)
    return (d_query, d_keys, d_values, loss_sum)


def fold_values(value_rows, disc_heads):
    head_count = disc_heads.shape[0]
    value_heads = value_rows.astype(jnp.float32).reshape(value_rows.shape[0], head_count, HD)
    return jnp.einsum("rhd,hd->hr", value_heads, disc_heads, precision=exact_dots)


def shards(latents, noise, steps, layout, w_time, w_student, w_qk, w_value, w_disc):
    channels = latents.shape[1]
    block_len = noise.shape[0]
    rows_each, col_count = w_student.shape
    head_count = w_value.shape[1] // HD
    shard_fold = fold_values(w_value, w_disc.reshape(head_count, HD))
    fold_tile = jnp.pad(shard_fold, ((0, 8 - head_count), (0, 128 - rows_each)))
    ws_all, wqk_all, fold_all, lat_all = gather_all(w_student, w_qk, fold_tile, latents)
    student_weights = ws_all.reshape(channels, col_count)
    qk_weights = wqk_all.reshape(channels, w_qk.shape[1])
    folded = (
        fold_all[..., :head_count, :rows_each]
        .reshape(-1, head_count, rows_each)
        .transpose(0, 2, 1)
        .reshape(channels, head_count)
    )
    clip_tokens = lat_all.reshape(block_len, channels)
    col_start = lax.axis_index("ctx") * col_count
    clip_index = lax.axis_index("dp")
    step_now = lax.dynamic_slice_in_dim(steps, clip_index, 1, 0)
    modulation = jnp.dot(time_embedding(step_now), w_time, preferred_element_type=jnp.float32)[0]
    shift_mod = modulation[:channels]
    scale_mod = modulation[channels : 2 * channels]
    gate_mod = modulation[2 * channels :]
    gate_cols = lax.dynamic_slice_in_dim(gate_mod, col_start, col_count, 0)
    sigma_clip = 0.25 + 0.5 * step_now.astype(jnp.float32)[0] / STEPS
    normed, unused_inverse = normalize(clip_tokens.astype(jnp.float32))
    mod_in = (normed * (1.0 + scale_mod) + shift_mod).astype(jnp.bfloat16)
    branch = jnp.dot(mod_in, student_weights, preferred_element_type=jnp.float32)
    own_cols = lax.dynamic_slice_in_dim(clip_tokens, col_start, col_count, 1).astype(jnp.float32)
    student_cols = own_cols + gate_cols * branch
    teacher_part = (
        (1.0 - sigma_clip) * student_cols + sigma_clip * noise.astype(jnp.float32)
    ).astype(jnp.bfloat16)
    teacher_in = teacher_gather(teacher_part)
    tnorm, inverse = normalize(teacher_in.astype(jnp.float32))
    tnorm_b = tnorm.astype(jnp.bfloat16)
    qk_proj = jnp.dot(tnorm_b, qk_weights, preferred_element_type=jnp.float32).reshape(
        block_len, head_count, 2, HD
    )
    cosine, sine_tab = rotary_tables(layout[0])
    query_rot = rotate(qk_proj[:, :, 0], cosine, sine_tab).astype(jnp.bfloat16)
    key_rot = rotate(qk_proj[:, :, 1], cosine, sine_tab).astype(jnp.bfloat16)
    values_b = jnp.dot(
        tnorm_b, folded, precision=exact_dots, preferred_element_type=jnp.float32
    ).astype(jnp.bfloat16)
    d_query, d_keys, d_values, loss_sum = attend(query_rot, key_rot, values_b, block_len)
    d_key_own = lax.optimization_barrier(d_keys.astype(jnp.bfloat16)).astype(jnp.float32)
    d_values_own = lax.optimization_barrier(d_values.astype(jnp.bfloat16)).astype(jnp.float32)
    d_qk = jnp.stack(
        [unrotate(d_query, cosine, sine_tab), unrotate(d_key_own, cosine, sine_tab)], axis=2
    )
    d_qk = d_qk.reshape(block_len, head_count * 2 * HD).astype(jnp.bfloat16)
    d_part = lax.dot_general(
        d_qk, qk_weights, (((1,), (1,)), ((), ())), preferred_element_type=jnp.float32
    )
    d_part = d_part + lax.dot_general(
        d_values_own,
        folded,
        (((1,), (1,)), ((), ())),
        precision=exact_dots,
        preferred_element_type=jnp.float32,
    )
    sums = jnp.stack([jnp.sum(d_part, axis=1), jnp.sum(d_part * tnorm, axis=1)])
    d_tnorm, sums = reduce_clip(d_part, jnp.pad(sums, ((0, 6), (0, 0))))
    mean_d = (sums[0] / channels)[:, None]
    mean_dt = (sums[1] / channels)[:, None]
    tnorm_cols = lax.dynamic_slice_in_dim(tnorm, col_start, col_count, 1)
    d_cols = inverse * (d_tnorm - mean_d - tnorm_cols * mean_dt)
    d_branch = (gate_cols * (1.0 - sigma_clip) * d_cols).astype(jnp.bfloat16)
    grad_part = lax.dot_general(
        mod_in, d_branch, (((0,), (0,)), ((), ())), preferred_element_type=jnp.float32
    ).astype(jnp.bfloat16)
    lanes = lax.broadcasted_iota(jnp.int32, (8, 128), 1)
    loss_tile = jnp.where(lanes == clip_index, loss_sum / block_len, jnp.float32(0.0))
    student_grad, losses = scatter_all(
        grad_part.reshape(4, 4, 4, rows_each, col_count), loss_tile
    )
    clip_loss = losses[0, : steps.shape[0]]
    return (clip_loss, student_grad)


def solution(mesh):
    return jax.shard_map(
        shards,
        mesh=mesh,
        in_specs=(
            P(("dp", "ctx"), None),
            P("dp", "ctx"),
            P(),
            P("dp", None),
            P(),
            P("dp", "ctx"),
            P("dp", "ctx"),
            P("dp", "ctx"),
            P("ctx"),
        ),
        out_specs=(P(), P("dp", "ctx")),
        check_vma=False,
    )
```

```python
import functools
import math

import jax
import jax.numpy as jnp
from jax import lax
from jax.experimental import pallas as pl
from jax.experimental.pallas import tpu as pltpu
from jax.sharding import PartitionSpec as P

HD = 128
FREQ = 256
STEPS = 1000
MESH = pl.DeviceIdType.MESH
VMEM = pltpu.VMEM
VSPEC = pl.BlockSpec(memory_space=pltpu.VMEM)
ASPEC = pl.BlockSpec(memory_space=pl.ANY)
F32 = jnp.float32
BF16 = jnp.bfloat16


ln_eps = 1e-06
exact_dots = lax.Precision.HIGHEST


def place():
    d = lax.axis_index("dp")
    c = lax.axis_index("ctx")
    return d // 16, (d // 4) % 4, d % 4, c // 2, c % 2


class Links:
    def __init__(self, send_sems, recv_sems):
        self.send_sems, self.recv_sems = send_sems, recv_sems
        self.used = 0
        self.open = []
        self.zh, self.x, self.y, self.zl, self.core = place()

    def dev(self, zh=0, x=0, y=0, zl=0, core=0):
        z_new = (self.zh + zh) % 4
        x_new = (self.x + x) % 4
        y_new = (self.y + y) % 4
        return (
            z_new * 16 + x_new * 4 + y_new,
            ((self.zl + zl) % 2) * 2 + (self.core + core) % 2,
        )

    def barrier(self, steps):
        sem = pltpu.get_barrier_semaphore()
        for step in steps:
            pl.semaphore_signal(sem, inc=1, device_id=self.dev(**step), device_id_type=MESH)
        pl.semaphore_wait(sem, len(steps))

    def send(self, src, dst, **step):
        slot = self.used
        self.used += 1
        copy = pltpu.make_async_remote_copy(
            src_ref=src,
            dst_ref=dst,
            send_sem=self.send_sems.at[slot],
            recv_sem=self.recv_sems.at[slot],
            device_id=self.dev(**step),
            device_id_type=MESH,
        )
        copy.start()
        self.open.append(copy)
        return copy

    def drain(self):
        for copy in self.open:
            copy.wait_send()


AXES_AB = (("x", "y", 0), ("y", "x", 2))


def slot_of(links, axis, step, other=None, zs=slice(0, 2)):
    moved = {"x": links.x, "y": links.y}
    moved[axis] = (moved[axis] + step) % 4
    picks = dict(moved)
    if other is not None:
        picks[other] = slice(None)
    return (zs, picks["x"], picks["y"])


class Gather:
    def __init__(self, links, shard, out, loc_sem):
        self.links, self.shard, self.out = links, shard, out
        self.own = pltpu.make_async_copy(shard, out.at[links.zh, links.x, links.y], loc_sem)

    def along_z(self):
        links = self.links
        self.own.start()
        home = self.out.at[links.zh, links.x, links.y]
        self.copies = [links.send(self.shard, home, zh=step) for step in (1, 3, 2)]

    def settle(self):
        for copy in self.copies:
            copy.wait_recv()
        self.copies = []

    def spread(self, second):
        links = self.links
        if not second:
            self.own.wait()
        self.settle()
        self.near = []
        for first_axis, second_axis, base in AXES_AB:
            axis = second_axis if second else first_axis
            other = first_axis if second else None
            mine = self.out.at[slot_of(links, axis, 0, other, slice(base, base + 2))]
            self.near.append(
                (
                    axis,
                    other,
                    base,
                    links.send(mine, mine, **{axis: 1}),
                    links.send(mine, mine, **{axis: 3}),
                )
            )

    def relay(self):
        links = self.links
        self.copies = []
        for axis, other, base, up, down in self.near:
            up.wait_recv()
            piece = self.out.at[slot_of(links, axis, 3, other, base)]
            self.copies.append(links.send(piece, piece, **{axis: 1}))
            down.wait_recv()
            piece = self.out.at[slot_of(links, axis, 1, other, base + 1)]
            self.copies.append(links.send(piece, piece, **{axis: 3}))


NEAR = (
    dict(core=1),
    dict(zl=1),
    dict(zl=1, core=1),
    dict(zh=1),
    dict(zh=2),
    dict(zh=3),
    dict(x=1),
    dict(x=2),
    dict(x=3),
    dict(y=1),
    dict(y=2),
    dict(y=3),
)
CLIP_ALL = NEAR[:3]


class Scatter:
    def __init__(self, links, axis, read, plain, bufs):
        self.links, self.axis, self.read, self.plain = links, axis, read, plain
        self.one_up, self.one_down, self.mix_up, self.mix_down, self.two_up, self.two_down = bufs
        self.last = []

    def start(self, half):
        links, axis, plain = self.links, self.axis, self.plain
        if half == 0:
            self.up = links.send(plain(0, 2), self.one_up, **{axis: 1})
            self.last.append(links.send(plain(0, 3), self.two_down.at[0], **{axis: 3}))
        else:
            self.down = links.send(plain(1, 2), self.one_down, **{axis: 3})
            self.last.append(links.send(plain(1, 1), self.two_up.at[1], **{axis: 1}))

    def middle(self):
        links, axis = self.links, self.axis
        self.up.wait_recv()
        self.mix_up[...] = (self.read(0, 1) + self.one_up[...].astype(F32)).astype(BF16)
        self.last.append(links.send(self.mix_up, self.two_up.at[0], **{axis: 1}))
        self.down.wait_recv()
        self.mix_down[...] = (self.read(1, 3) + self.one_down[...].astype(F32)).astype(BF16)
        self.last.append(links.send(self.mix_down, self.two_down.at[1], **{axis: 3}))

    def finish(self, store):
        for copy in self.last:
            copy.wait_recv()
        for half in range(2):
            store(
                half,
                self.read(half, 0)
                + self.two_up[half].astype(F32)
                + self.two_down[half].astype(F32),
            )


def dot(a, b):
    return jnp.dot(a, b, preferred_element_type=F32)


def dot_t(a, b):
    return lax.dot_general(a, b, (((1,), (1,)), ((), ())), preferred_element_type=F32)


def lanes_of(row, count):
    return jnp.transpose(jnp.broadcast_to(row[0:1], (128, count)))


def step_body(
    lat, noise, steps, layout, w_time, ws, wqk, wv, disc,
    grad_o, loss_o,
    send_sems, recv_sems, loc_sems,
    wt, wx, ws_all, wx_all, lat_all, mod, modin, mod_t, part, tin, mean_c, inv_c,
    tables, qk, q_t, probs, pv, vrow, logit_s, logit_r, dlog, d_sc, dv_t, dqk,
    stage, from_core, cross, from_chip, own, sums, stats_s, stats_r, dbr,
    loss_buf, loss_mid, z_send, z_recv, z_keep, *bufs,
):
    links = Links(send_sems, recv_sems)
    tokens, cols = noise.shape
    channels = lat.shape[1]
    rows_each = lat.shape[0]
    heads = cols // HD
    dp, zl, core = lax.axis_index("dp"), links.zl, links.core
    me = zl * 2 + core
    beside_me = zl * 2 + (core + 1) % 2
    far = ((zl + 1) % 2) * 2 + core
    far_beside = ((zl + 1) % 2) * 2 + (core + 1) % 2
    fold_at = 2 * cols

    def col(owner, base=0):
        return pl.ds(pl.multiple_of(base + owner * cols, 128), cols)

    get_wt = pltpu.make_async_copy(w_time, wt, loc_sems.at[0])
    get_wt.start()
    links.barrier(NEAR)
    g_ws = Gather(links, ws, ws_all, loc_sems.at[1])
    g_wx = Gather(links, wx, wx_all, loc_sems.at[2])
    g_ws.along_z()

    lane = lax.broadcasted_iota(jnp.int32, (ws.shape[0], 128), 1)
    scaled = wv[...].astype(F32) * disc[...]
    extra = jnp.zeros((ws.shape[0], 128), F32)
    for head in range(heads):
        value = jnp.sum(scaled[:, head * HD : (head + 1) * HD], axis=1, keepdims=True)
        for term in range(3):
            piece = value.astype(BF16).astype(F32)
            extra = jnp.where(lane == term * 8 + head, piece, extra)
            value = value - piece
    wx[:, :fold_at] = wqk[...]
    wx[:, fold_at:] = extra.astype(BF16)
    g_wx.along_z()

    step_f = jnp.full((8, 128), steps[dp], jnp.int32).astype(F32)
    spot = lax.broadcasted_iota(jnp.int32, (8, 128), 1).astype(F32)
    angle = step_f * jnp.exp(-math.log(10000.0) * spot / (FREQ // 2))
    embed = jnp.concatenate([jnp.cos(angle), jnp.sin(angle)], axis=1).astype(BF16)
    sigma = (0.25 + 0.5 * step_f / STEPS)[0:1, 0:1]
    get_wt.wait()
    for third in range(3):
        here = slice(third * channels, (third + 1) * channels)
        mod[:, here] = dot(embed, wt[:, here])

    g_ws.spread(False)
    own_lat = pltpu.make_async_copy(lat, lat_all.at[me], loc_sems.at[3])
    own_lat.start()
    halves = [slice(0, rows_each // 2), slice(rows_each // 2, rows_each)]
    across = [links.send(lat.at[h], lat_all.at[me, h], zl=1) for h in halves]
    beside = links.send(lat, lat_all.at[me], core=1)

    def norm_rows(owner):
        def rows16(index, carry):
            rows = pl.ds(pl.multiple_of(index * 16, 16), 16)
            value = lat_all[owner, rows].astype(F32)
            value = value - jnp.sum(value, axis=1, keepdims=True) * (1.0 / channels)
            spread = jnp.sum(value * value, axis=1, keepdims=True) * (1.0 / channels)
            value = value * lax.rsqrt(spread + ln_eps)
            value = value * (1.0 + mod[0:1, channels : 2 * channels]) + mod[0:1, :channels]
            modin[pl.ds(pl.multiple_of(owner * rows_each + index * 16, 16), 16)] = value.astype(BF16)
            return carry

        lax.fori_loop(0, rows_each // 16, rows16, 0)

    own_lat.wait()
    norm_rows(me)
    g_ws.relay()
    g_ws.spread(True)
    g_wx.spread(False)
    beside.wait_recv()
    norm_rows(beside_me)
    g_ws.relay()
    g_wx.relay()
    g_wx.spread(True)
    passed = []
    for copy, h in zip(across, halves):
        copy.wait_recv()
        passed.append(links.send(lat_all.at[far, h], lat_all.at[far, h], core=1))
    norm_rows(far)
    for copy in passed:
        copy.wait_recv()
    norm_rows(far_beside)

    def flip(index, carry):
        here = pl.ds(pl.multiple_of(index * 128, 128), 128)
        mod_t[here] = jnp.transpose(modin[:, here].astype(F32)).astype(BF16)
        return carry

    g_ws.settle()
    gate = mod[0:1, col(me, 2 * channels)]
    keep = 1.0 - sigma
    size = tokens // 2
    sent, near = [], []
    for index in range(2):
        rows = pl.ds(index * size, size)
        branch = dot(modin[rows], ws_all[...].reshape(channels, cols))
        mine = lat_all[pl.ds(index * 2, 2), :, col(me)].reshape(size, cols).astype(F32)
        mixed = keep * (mine + gate * branch) + sigma * noise[rows].astype(F32)
        part[rows] = mixed.astype(BF16)
        sent.append(links.send(part.at[rows], tin.at[rows, col(me)], zl=1))
        near.append(links.send(part.at[rows], tin.at[rows, col(me)], core=1))
        tin[rows, col(me)] = mixed.astype(BF16)
    g_wx.relay()
    lax.fori_loop(0, channels // 128, flip, 0)

    place_c = lanes_of(layout[...].astype(F32), tokens)
    lane = lax.broadcasted_iota(jnp.int32, (tokens, 128), 1)
    omega = jnp.exp(-math.log(10000.0) * (lane % 64).astype(F32) / 64)
    tables[0] = jnp.cos(place_c * omega)
    sine = jnp.sin(place_c * omega)
    tables[1] = jnp.where(lane < 64, -sine, sine)

    passed = []
    for index in range(2):
        rows = pl.ds(index * size, size)
        sent[index].wait_recv()
        passed.append(links.send(tin.at[rows, col(far)], tin.at[rows, col(far)], core=1))
    tnorm_b = modin
    for index in range(2):
        near[index].wait_recv()
        passed[index].wait_recv()

        def rows16(step, carry):
            rows = pl.ds(pl.multiple_of(index * size + step * 16, 16), 16)
            value = tin[rows].astype(F32)
            mean = jnp.sum(value, axis=1, keepdims=True) * (1.0 / channels)
            value = value - mean
            spread = jnp.sum(value * value, axis=1, keepdims=True) * (1.0 / channels)
            inverse = lax.rsqrt(spread + ln_eps)
            tnorm_b[rows] = (value * inverse).astype(BF16)
            mean_c[rows] = jnp.broadcast_to(mean, (16, 128))
            inv_c[rows] = jnp.broadcast_to(inverse, (16, 128))
            return carry

        lax.fori_loop(0, size // 16, rows16, 0)
    g_wx.settle()
    links.drain()
    links.open = []

    def project(head, carry):
        weights = wx_all[:, :, :, :, pl.ds(pl.multiple_of(head * 256, 256), 256)]
        both = dot(tnorm_b[...], weights.reshape(channels, 256))
        cosine, sine = tables[0], tables[1]
        query, key = both[:, :HD], both[:, HD:]
        query = query * cosine + pltpu.roll(query, 64, 1) * sine
        key = key * cosine + pltpu.roll(key, 64, 1) * sine
        qk[:, pl.ds(pl.multiple_of(head * 256, 256), 128)] = query.astype(BF16)
        qk[:, pl.ds(pl.multiple_of(head * 256 + 128, 128), 128)] = key.astype(BF16)
        q_t[head] = jnp.transpose(query).astype(BF16)
        return carry

    lax.fori_loop(0, heads, project, 0)
    value_t = jnp.transpose(
        dot(tnorm_b[...], wx_all[:, :, :, :, pl.ds(fold_at, 128)].reshape(channels, 128))
    )
    vrow[...] = (value_t[0:8] + value_t[8:16] + value_t[16:24]).astype(BF16).astype(F32)

    scale_dot = 1.0 / math.sqrt(HD)
    block = 128
    blocks = tokens // block

    def attend(trip, carry):
        head, index = trip // blocks, trip % blocks
        rows = pl.ds(pl.multiple_of(index * block, block), block)
        query = qk[rows, pl.ds(pl.multiple_of(head * 256, 256), 128)]
        key = qk[:, pl.ds(pl.multiple_of(head * 256 + 128, 128), 128)]
        scores = dot_t(query, key) * scale_dot
        weights = jnp.exp(scores - jnp.max(scores, axis=1, keepdims=True))
        weights = weights * (1.0 / jnp.sum(weights, axis=1, keepdims=True))
        probs[head, rows] = weights
        share = jnp.sum(weights * vrow[pl.ds(head, 1)], axis=1, keepdims=True)
        pv[head, rows] = jnp.broadcast_to(share, (block, 128))
        return carry

    lax.fori_loop(0, heads * blocks, attend, 0)
    total = pv[0]
    for head in range(1, heads):
        total = total + pv[head]
    logit_s[...] = jnp.transpose(total)[0:8]
    tiny = [links.send(logit_s, logit_r.at[i], **step) for i, step in enumerate(CLIP_ALL)]
    dv_t[...] = jnp.zeros_like(dv_t)
    for copy in tiny:
        copy.wait_recv()
    logit = logit_s[...] + logit_r[0] + logit_r[1] + logit_r[2]
    soft = jnp.maximum(-logit, 0.0) + jnp.log1p(jnp.exp(-jnp.abs(logit)))
    loss = jnp.sum(soft, axis=1, keepdims=True) * (1.0 / tokens)
    lane = lax.broadcasted_iota(jnp.int32, (8, 128), 1)
    loss_mid[0] = jnp.where(lane == dp, jnp.broadcast_to(loss, (8, 128)), 0.0)

    def loss_step(index, axis):
        return [
            links.send(loss_mid.at[index], loss_buf.at[index, step - 1], **{axis: step})
            for step in (1, 2, 3)
        ]

    def loss_sum(index, copies):
        for copy in copies:
            copy.wait_recv()
        return loss_mid[index] + loss_buf[index, 0] + loss_buf[index, 1] + loss_buf[index, 2]

    tiny = loss_step(0, "y")
    dlog[...] = lanes_of((-1.0 / tokens) / (1.0 + jnp.exp(logit)), tokens)

    def backward(head, carry):
        def rows_of(index, d_value):
            rows = pl.ds(pl.multiple_of(index * block, block), block)
            weights = probs[head, rows]
            slope = dlog[rows][:, 0:1]
            tilt = vrow[pl.ds(head, 1)] - pv[head, rows][:, 0:1]
            d_sc[rows] = (weights * tilt * (slope * scale_dot)).astype(BF16)
            return d_value + jnp.sum(weights * slope, axis=0, keepdims=True)

        d_value = lax.fori_loop(0, blocks, rows_of, jnp.zeros((1, tokens), F32))
        d_value = d_value.astype(BF16).astype(F32)
        for term in range(3):
            dv_t[pl.ds(term * 8 + head, 1)] = d_value
        key = qk[:, pl.ds(pl.multiple_of(head * 256 + 128, 128), 128)]
        cosine, sine = tables[0], tables[1]
        d_query = dot(d_sc[...], key)
        d_key = jnp.transpose(dot(q_t[head], d_sc[...])).astype(BF16).astype(F32)
        d_query = d_query * cosine - pltpu.roll(d_query, 64, 1) * sine
        d_key = d_key * cosine - pltpu.roll(d_key, 64, 1) * sine
        dqk[:, pl.ds(pl.multiple_of(head * 256, 256), 128)] = d_query.astype(BF16)
        dqk[:, pl.ds(pl.multiple_of(head * 256 + 128, 128), 128)] = d_key.astype(BF16)
        return carry

    lax.fori_loop(0, heads, backward, 0)
    dqk[:, fold_at:] = jnp.transpose(dv_t[...]).astype(BF16)
    loss_mid[1] = loss_sum(0, tiny)
    tiny = loss_step(1, "x")

    sums[...] = jnp.zeros_like(sums)

    def d_block(owner, rows):
        weights = wx_all[owner].reshape(cols, wx.shape[1])
        value = dot_t(dqk[rows], weights)
        normed = (tin[rows, col(owner)].astype(F32) - mean_c[rows][:, 0:1]) * inv_c[rows][:, 0:1]
        sums[0, rows] = sums[0, rows] + jnp.sum(value, axis=1, keepdims=True)
        sums[1, rows] = sums[1, rows] + jnp.sum(value * normed, axis=1, keepdims=True)
        return value

    pieces = [pl.ds(index * size, size) for index in range(2)]
    first, second, third = [], [], []
    for rows in pieces:
        stage[1, rows] = d_block(far_beside, rows).astype(BF16)
        first.append(links.send(stage.at[1, rows], from_core.at[1, rows], core=1))
    for index, rows in enumerate(pieces):
        value = d_block(far, rows)
        first[index].wait_recv()
        cross[rows] = (value + from_core[1, rows].astype(F32)).astype(BF16)
        second.append(links.send(cross.at[rows], from_chip.at[rows], zl=1))
    for rows in pieces:
        stage[0, rows] = d_block(beside_me, rows).astype(BF16)
        third.append(links.send(stage.at[0, rows], from_core.at[0, rows], core=1))
    for rows in pieces:
        own[rows] = d_block(me, rows)
    loss_mid[2] = loss_sum(1, tiny)
    tiny = loss_step(2, "zh")
    stats_s[0:8] = jnp.transpose(sums[0])[0:8]
    stats_s[8:16] = jnp.transpose(sums[1])[0:8]
    stats = [links.send(stats_s, stats_r.at[i], **step) for i, step in enumerate(CLIP_ALL)]
    for copy in stats:
        copy.wait_recv()
    both = (stats_s[...] + stats_r[0] + stats_r[1] + stats_r[2]) * (1.0 / channels)
    sums[0] = lanes_of(both[0:8], tokens)
    sums[1] = lanes_of(both[8:16], tokens)
    for index, rows in enumerate(pieces):
        third[index].wait_recv()
        second[index].wait_recv()
        value = own[rows] + from_core[0, rows].astype(F32) + from_chip[rows].astype(F32)
        inverse = inv_c[rows][:, 0:1]
        normed = (tin[rows, col(me)].astype(F32) - mean_c[rows][:, 0:1]) * inverse
        value = inverse * (value - sums[0, rows][:, 0:1] - normed * sums[1, rows][:, 0:1])
        dbr[rows] = (gate * keep * value).astype(BF16)

    grads = ws_all
    spare = list(bufs)
    stages = []
    for first_axis, second_axis, base in (("y", "x", 0), ("x", "y", 2)):
        big, spare = spare[:6], spare[6:]
        small, spare = spare[:6], spare[6:]
        mid, mid_b, spare = spare[0], spare[1], spare[2:]

        def plain1(half, step, axis=first_axis, other=second_axis, base=base):
            return grads.at[slot_of(links, axis, step, other, base + half)]

        def read1(half, step, plain=plain1):
            return plain(half, step)[...].astype(F32)

        def spot_of(step, axis=second_axis):
            return ({"x": links.x, "y": links.y}[axis] + step) % 4

        def plain2(half, step, mid_b=mid_b, spot=spot_of):
            return mid_b.at[half, spot(step)]

        def read2(half, step, mid=mid, spot=spot_of):
            return mid[half, spot(step)]

        stages.append(
            (
                base,
                mid,
                mid_b,
                Scatter(links, first_axis, read1, plain1, big),
                Scatter(links, second_axis, read2, plain2, small),
            )
        )
    for quarter in (0, 2, 1, 3):
        here = pl.ds(quarter * cols, cols)
        value = dot(mod_t[here], dbr[...]).astype(BF16)
        grads[quarter] = value.reshape(grads.shape[1:])
        stages[quarter // 2][3].start(quarter % 2)
    for pair in stages:
        pair[3].middle()
    for base, mid, mid_b, first_ring, second_ring in stages:

        def store(half, value, mid=mid, mid_b=mid_b):
            mid[half] = value
            mid_b[half] = value.astype(BF16)

        first_ring.finish(store)
        second_ring.start(0)
        second_ring.start(1)
    for pair in stages:
        pair[4].middle()
    for base, mid, mid_b, first_ring, second_ring in stages:

        def hold(half, value, base=base):
            z_keep[base + half] = value
            z_send[base + half] = value.astype(BF16)

        second_ring.finish(hold)
    tail = [
        links.send(z_send.at[(links.zh + step) % 4], z_recv.at[step - 1], zh=step)
        for step in (1, 3, 2)
    ]
    loss_o[...] = loss_sum(2, tiny)
    for copy in tail:
        copy.wait_recv()
    grad_o[...] = (
        z_keep[links.zh]
        + z_recv[0].astype(F32)
        + z_recv[1].astype(F32)
        + z_recv[2].astype(F32)
    )
    links.drain()


def shards(latents, noise, steps, layout, w_time, w_student, w_qk, w_value, w_disc):
    channels = latents.shape[1]
    tokens, cols = noise.shape
    rows = w_student.shape[0]
    heads = cols // HD
    wide = w_qk.shape[1] + 128
    big = [VMEM((4, rows, cols), BF16)] * 4 + [VMEM((2, 4, rows, cols), BF16)] * 2
    small = [VMEM((rows, cols), BF16)] * 4 + [VMEM((2, rows, cols), BF16)] * 2
    mids = [VMEM((2, 4, rows, cols), F32), VMEM((2, 4, rows, cols), BF16)]
    scratch = [
        pltpu.SemaphoreType.DMA((128,)),
        pltpu.SemaphoreType.DMA((128,)),
        pltpu.SemaphoreType.DMA((4,)),
        VMEM(w_time.shape, BF16),
        VMEM((rows, wide), BF16),
        VMEM((4, 4, 4, rows, cols), BF16),
        VMEM((4, 4, 4, rows, wide), BF16),
        VMEM((4,) + latents.shape, BF16),
        VMEM((8, w_time.shape[1]), F32),
        VMEM((tokens, channels), BF16),
        VMEM((channels, tokens), BF16),
        VMEM((tokens, cols), BF16),
        VMEM((tokens, channels), BF16),
        VMEM((tokens, 128), F32),
        VMEM((tokens, 128), F32),
        VMEM((2, tokens, 128), F32),
        VMEM((tokens, 2 * cols), BF16),
        VMEM((heads, HD, tokens), BF16),
        VMEM((heads, tokens, tokens), F32),
        VMEM((heads, tokens, 128), F32),
        VMEM((8, tokens), F32),
        VMEM((8, tokens), F32),
        VMEM((3, 8, tokens), F32),
        VMEM((tokens, 128), F32),
        VMEM((tokens, tokens), BF16),
        VMEM((128, tokens), F32),
        VMEM((tokens, wide), BF16),
        VMEM((2, tokens, cols), BF16),
        VMEM((2, tokens, cols), BF16),
        VMEM((tokens, cols), BF16),
        VMEM((tokens, cols), BF16),
        VMEM((tokens, cols), F32),
        VMEM((2, tokens, 128), F32),
        VMEM((16, tokens), F32),
        VMEM((3, 16, tokens), F32),
        VMEM((tokens, cols), BF16),
        VMEM((3, 3, 8, 128), F32),
        VMEM((3, 8, 128), F32),
        VMEM((4, rows, cols), BF16),
        VMEM((3, rows, cols), BF16),
        VMEM((4, rows, cols), F32),
    ] + (big + small + mids) * 2
    student_grad, losses = pl.pallas_call(
        step_body,
        out_shape=(
            jax.ShapeDtypeStruct((rows, cols), F32),
            jax.ShapeDtypeStruct((8, 128), F32),
        ),
        in_specs=[
            VSPEC,
            VSPEC,
            pl.BlockSpec(memory_space=pltpu.SMEM),
            VSPEC,
            ASPEC,
            VSPEC,
            VSPEC,
            VSPEC,
            VSPEC,
        ],
        out_specs=(VSPEC, VSPEC),
        scratch_shapes=scratch,
        compiler_params=pltpu.CompilerParams(
            collective_id=1, has_side_effects=True, vmem_limit_bytes=67043328
        ),
    )(latents, noise, steps, layout, w_time, w_student, w_qk, w_value, w_disc.reshape(1, cols))
    return (losses[0, : steps.shape[0]], student_grad)


def solution(mesh):
    return jax.shard_map(
        shards,
        mesh=mesh,
        in_specs=(
            P(("dp", "ctx"), None),
            P("dp", "ctx"),
            P(),
            P("dp", None),
            P(),
            P("dp", "ctx"),
            P("dp", "ctx"),
            P("dp", "ctx"),
            P("ctx"),
        ),
        out_specs=(P(), P("dp", "ctx")),
        check_vma=False,
    )
```

```python
import functools
import math

import jax
import jax.numpy as jnp
from jax import lax
from jax.experimental import pallas as pl
from jax.experimental.pallas import tpu as pltpu
from jax.sharding import PartitionSpec as P

HD = 128
FREQ = 256
STEPS = 1000
MESH = pl.DeviceIdType.MESH
VMEM = pltpu.VMEM
VSPEC = pl.BlockSpec(memory_space=pltpu.VMEM)
ASPEC = pl.BlockSpec(memory_space=pl.ANY)
F32 = jnp.float32
BF16 = jnp.bfloat16


ln_eps = 1e-06
exact_dots = lax.Precision.HIGHEST


def place():
    d = lax.axis_index("dp")
    c = lax.axis_index("ctx")
    return d // 16, (d // 4) % 4, d % 4, c // 2, c % 2


class Links:
    def __init__(self, send_sems, recv_sems):
        self.send_sems, self.recv_sems = send_sems, recv_sems
        self.used = 0
        self.open = []
        self.zh, self.x, self.y, self.zl, self.core = place()

    def dev(self, zh=0, x=0, y=0, zl=0, core=0):
        z_new = (self.zh + zh) % 4
        x_new = (self.x + x) % 4
        y_new = (self.y + y) % 4
        return (
            z_new * 16 + x_new * 4 + y_new,
            ((self.zl + zl) % 2) * 2 + (self.core + core) % 2,
        )

    def barrier(self, steps):
        sem = pltpu.get_barrier_semaphore()
        for step in steps:
            pl.semaphore_signal(sem, inc=1, device_id=self.dev(**step), device_id_type=MESH)
        pl.semaphore_wait(sem, len(steps))

    def send(self, src, dst, **step):
        slot = self.used
        self.used += 1
        copy = pltpu.make_async_remote_copy(
            src_ref=src,
            dst_ref=dst,
            send_sem=self.send_sems.at[slot],
            recv_sem=self.recv_sems.at[slot],
            device_id=self.dev(**step),
            device_id_type=MESH,
        )
        copy.start()
        self.open.append(copy)
        return copy

    def drain(self):
        for copy in self.open:
            copy.wait_send()


AXES_AB = (("x", "y", 0), ("y", "x", 2))


def slot_of(links, axis, step, other=None, zs=slice(0, 2)):
    moved = {"x": links.x, "y": links.y}
    moved[axis] = (moved[axis] + step) % 4
    picks = dict(moved)
    if other is not None:
        picks[other] = slice(None)
    return (zs, picks["x"], picks["y"])


class Gather:
    def __init__(self, links, shard, out, loc_sem):
        self.links, self.shard, self.out = links, shard, out
        self.own = pltpu.make_async_copy(shard, out.at[links.zh, links.x, links.y], loc_sem)

    def along_z(self):
        links = self.links
        self.own.start()
        home = self.out.at[links.zh, links.x, links.y]
        self.copies = [links.send(self.shard, home, zh=step) for step in (1, 3, 2)]

    def settle(self):
        for copy in self.copies:
            copy.wait_recv()
        self.copies = []

    def spread(self, second):
        links = self.links
        if not second:
            self.own.wait()
        self.settle()
        self.near = []
        for first_axis, second_axis, base in AXES_AB:
            axis = second_axis if second else first_axis
            other = first_axis if second else None
            mine = self.out.at[slot_of(links, axis, 0, other, slice(base, base + 2))]
            self.near.append(
                (
                    axis,
                    other,
                    base,
                    links.send(mine, mine, **{axis: 1}),
                    links.send(mine, mine, **{axis: 3}),
                )
            )

    def relay(self):
        links = self.links
        self.copies = []
        for axis, other, base, up, down in self.near:
            up.wait_recv()
            piece = self.out.at[slot_of(links, axis, 3, other, base)]
            self.copies.append(links.send(piece, piece, **{axis: 1}))
            down.wait_recv()
            piece = self.out.at[slot_of(links, axis, 1, other, base + 1)]
            self.copies.append(links.send(piece, piece, **{axis: 3}))


NEAR = (
    dict(core=1),
    dict(zl=1),
    dict(zl=1, core=1),
    dict(zh=1),
    dict(zh=2),
    dict(zh=3),
    dict(x=1),
    dict(x=2),
    dict(x=3),
    dict(y=1),
    dict(y=2),
    dict(y=3),
)
CLIP_ALL = NEAR[:3]


class Scatter:
    def __init__(self, links, axis, read, plain, bufs):
        self.links, self.axis, self.read, self.plain = links, axis, read, plain
        self.one_up, self.one_down, self.mix_up, self.mix_down, self.two_up, self.two_down = bufs
        self.last = []

    def start(self, half):
        links, axis, plain = self.links, self.axis, self.plain
        if half == 0:
            self.up = links.send(plain(0, 2), self.one_up, **{axis: 1})
            self.last.append(links.send(plain(0, 3), self.two_down.at[0], **{axis: 3}))
        else:
            self.down = links.send(plain(1, 2), self.one_down, **{axis: 3})
            self.last.append(links.send(plain(1, 1), self.two_up.at[1], **{axis: 1}))

    def middle(self):
        links, axis = self.links, self.axis
        self.up.wait_recv()
        self.mix_up[...] = (self.read(0, 1) + self.one_up[...].astype(F32)).astype(BF16)
        self.last.append(links.send(self.mix_up, self.two_up.at[0], **{axis: 1}))
        self.down.wait_recv()
        self.mix_down[...] = (self.read(1, 3) + self.one_down[...].astype(F32)).astype(BF16)
        self.last.append(links.send(self.mix_down, self.two_down.at[1], **{axis: 3}))

    def finish(self, store):
        for copy in self.last:
            copy.wait_recv()
        for half in range(2):
            store(
                half,
                self.read(half, 0)
                + self.two_up[half].astype(F32)
                + self.two_down[half].astype(F32),
            )


def dot(a, b):
    return jnp.dot(a, b, preferred_element_type=F32)


def dot_t(a, b):
    return lax.dot_general(a, b, (((1,), (1,)), ((), ())), preferred_element_type=F32)


def lanes_of(row, count):
    return jnp.transpose(jnp.broadcast_to(row[0:1], (128, count)))


def step_body(
    lat, noise, steps, layout, w_time, ws, wqk, wv, disc,
    grad_o, loss_o,
    send_sems, recv_sems, loc_sems,
    wt, wx_1, wx_2, ws_all, wx_1_all, wx_2_all, lat_all, mod, modin, mod_t, part, tin, mean_c, inv_c,
    tables, qk, q_t, probs, pv, vrow, logit_s, logit_r, dlog, d_sc, dv_t, dqk,
    stage, from_core, cross, from_chip, own, sums, stats_s, stats_r, dbr,
    loss_buf, loss_mid, z_send, z_recv, z_keep, *bufs,
):
    links = Links(send_sems, recv_sems)
    tokens, cols = noise.shape
    channels = lat.shape[1]
    rows_each = lat.shape[0]
    heads = cols // HD
    dp, zl, core = lax.axis_index("dp"), links.zl, links.core
    me = zl * 2 + core
    beside_me = zl * 2 + (core + 1) % 2
    far = ((zl + 1) % 2) * 2 + core
    far_beside = ((zl + 1) % 2) * 2 + (core + 1) % 2
    early = (heads - 1) // 2
    fold_at = early * 2 * HD
    late_at = fold_at + 128

    def col(owner, base=0):
        return pl.ds(pl.multiple_of(base + owner * cols, 128), cols)

    get_wt = pltpu.make_async_copy(w_time, wt, loc_sems.at[0])
    get_wt.start()
    links.barrier(NEAR)
    g_ws = Gather(links, ws, ws_all, loc_sems.at[1])
    g_1 = Gather(links, wx_1, wx_1_all, loc_sems.at[2])
    g_2 = Gather(links, wx_2, wx_2_all, loc_sems.at[4])
    g_ws.along_z()

    lane = lax.broadcasted_iota(jnp.int32, (ws.shape[0], 128), 1)
    scaled = wv[...].astype(F32) * disc[...]
    extra = jnp.zeros((ws.shape[0], 128), F32)
    for head in range(heads):
        value = jnp.sum(scaled[:, head * HD : (head + 1) * HD], axis=1, keepdims=True)
        for term in range(3):
            piece = value.astype(BF16).astype(F32)
            extra = jnp.where(lane == term * 8 + head, piece, extra)
            value = value - piece
    wx_1[:, :fold_at] = wqk[:, :fold_at]
    wx_1[:, fold_at:] = extra.astype(BF16)
    wx_2[...] = wqk[:, fold_at:]
    g_1.along_z()

    step_f = jnp.full((8, 128), steps[dp], jnp.int32).astype(F32)
    spot = lax.broadcasted_iota(jnp.int32, (8, 128), 1).astype(F32)
    angle = step_f * jnp.exp(-math.log(10000.0) * spot / (FREQ // 2))
    embed = jnp.concatenate([jnp.cos(angle), jnp.sin(angle)], axis=1).astype(BF16)
    sigma = (0.25 + 0.5 * step_f / STEPS)[0:1, 0:1]
    g_ws.spread(False)
    own_lat = pltpu.make_async_copy(lat, lat_all.at[me], loc_sems.at[3])
    own_lat.start()
    halves = [slice(0, rows_each // 2), slice(rows_each // 2, rows_each)]
    across = [links.send(lat.at[h], lat_all.at[me, h], zl=1) for h in halves]
    beside = links.send(lat, lat_all.at[me], core=1)

    def norm_rows(owner):
        def rows16(index, carry):
            rows = pl.ds(pl.multiple_of(index * 16, 16), 16)
            value = lat_all[owner, rows].astype(F32)
            value = value - jnp.sum(value, axis=1, keepdims=True) * (1.0 / channels)
            spread = jnp.sum(value * value, axis=1, keepdims=True) * (1.0 / channels)
            value = value * lax.rsqrt(spread + ln_eps)
            value = value * (1.0 + mod[0:1, channels : 2 * channels]) + mod[0:1, :channels]
            modin[pl.ds(pl.multiple_of(owner * rows_each + index * 16, 16), 16)] = value.astype(BF16)
            return carry

        lax.fori_loop(0, rows_each // 16, rows16, 0)

    own_lat.wait()
    get_wt.wait()
    for third in range(3):
        here = slice(third * channels, (third + 1) * channels)
        mod[:, here] = dot(embed, wt[:, here])
    g_ws.relay()
    g_ws.spread(True)
    g_1.spread(False)
    g_2.along_z()
    norm_rows(me)
    beside.wait_recv()
    norm_rows(beside_me)
    g_ws.relay()
    g_1.relay()
    g_1.spread(True)
    passed = []
    for copy, h in zip(across, halves):
        copy.wait_recv()
        passed.append(links.send(lat_all.at[far, h], lat_all.at[far, h], core=1))
    norm_rows(far)
    g_2.spread(False)
    for copy in passed:
        copy.wait_recv()
    norm_rows(far_beside)

    def flip(index, carry):
        here = pl.ds(pl.multiple_of(index * 128, 128), 128)
        mod_t[here] = jnp.transpose(modin[:, here].astype(F32)).astype(BF16)
        return carry

    g_ws.settle()
    gate = mod[0:1, col(me, 2 * channels)]
    keep = 1.0 - sigma
    size = tokens // 2
    sent, near = [], []
    for index in range(2):
        rows = pl.ds(index * size, size)
        branch = dot(modin[rows], ws_all[...].reshape(channels, cols))
        mine = lat_all[pl.ds(index * 2, 2), :, col(me)].reshape(size, cols).astype(F32)
        mixed = keep * (mine + gate * branch) + sigma * noise[rows].astype(F32)
        part[rows] = mixed.astype(BF16)
        sent.append(links.send(part.at[rows], tin.at[rows, col(me)], zl=1))
        near.append(links.send(part.at[rows], tin.at[rows, col(me)], core=1))
        tin[rows, col(me)] = mixed.astype(BF16)
    g_1.relay()
    g_2.relay()
    g_2.spread(True)
    lax.fori_loop(0, channels // 128, flip, 0)

    place_c = lanes_of(layout[...].astype(F32), tokens)
    lane = lax.broadcasted_iota(jnp.int32, (tokens, 128), 1)
    omega = jnp.exp(-math.log(10000.0) * (lane % 64).astype(F32) / 64)
    tables[0] = jnp.cos(place_c * omega)
    sine = jnp.sin(place_c * omega)
    tables[1] = jnp.where(lane < 64, -sine, sine)

    passed = []
    for index in range(2):
        rows = pl.ds(index * size, size)
        sent[index].wait_recv()
        passed.append(links.send(tin.at[rows, col(far)], tin.at[rows, col(far)], core=1))
    tnorm_b = modin
    for index in range(2):
        near[index].wait_recv()
        passed[index].wait_recv()

        def rows16(step, carry):
            rows = pl.ds(pl.multiple_of(index * size + step * 16, 16), 16)
            value = tin[rows].astype(F32)
            mean = jnp.sum(value, axis=1, keepdims=True) * (1.0 / channels)
            value = value - mean
            spread = jnp.sum(value * value, axis=1, keepdims=True) * (1.0 / channels)
            inverse = lax.rsqrt(spread + ln_eps)
            tnorm_b[rows] = (value * inverse).astype(BF16)
            mean_c[rows] = jnp.broadcast_to(mean, (16, 128))
            inv_c[rows] = jnp.broadcast_to(inverse, (16, 128))
            return carry

        lax.fori_loop(0, size // 16, rows16, 0)
    g_1.settle()

    def project(head, source, base):
        weights = source[:, :, :, :, pl.ds(pl.multiple_of(head * 256 - base, 256), 256)]
        both = dot(tnorm_b[...], weights.reshape(channels, 256))
        cosine, sine = tables[0], tables[1]
        query, key = both[:, :HD], both[:, HD:]
        query = query * cosine + pltpu.roll(query, 64, 1) * sine
        key = key * cosine + pltpu.roll(key, 64, 1) * sine
        qk[:, pl.ds(pl.multiple_of(head * 256, 256), 128)] = query.astype(BF16)
        qk[:, pl.ds(pl.multiple_of(head * 256 + 128, 128), 128)] = key.astype(BF16)
        q_t[head] = jnp.transpose(query).astype(BF16)

    scale_dot = 1.0 / math.sqrt(HD)
    block = 128
    blocks = tokens // block

    def attend(trip, carry):
        head, index = trip // blocks, trip % blocks
        rows = pl.ds(pl.multiple_of(index * block, block), block)
        query = qk[rows, pl.ds(pl.multiple_of(head * 256, 256), 128)]
        key = qk[:, pl.ds(pl.multiple_of(head * 256 + 128, 128), 128)]
        scores = dot_t(query, key) * scale_dot
        weights = jnp.exp(scores - jnp.max(scores, axis=1, keepdims=True))
        weights = weights * (1.0 / jnp.sum(weights, axis=1, keepdims=True))
        probs[head, rows] = weights
        share = jnp.sum(weights * vrow[pl.ds(head, 1)], axis=1, keepdims=True)
        pv[head, rows] = jnp.broadcast_to(share, (block, 128))
        return carry

    def project_early(head, carry):
        project(head, wx_1_all, 0)
        return carry

    def project_late(head, carry):
        project(head, wx_2_all, fold_at)
        return carry

    lax.fori_loop(0, early, project_early, 0)
    value_t = jnp.transpose(
        dot(tnorm_b[...], wx_1_all[:, :, :, :, pl.ds(fold_at, 128)].reshape(channels, 128))
    )
    vrow[...] = (value_t[0:8] + value_t[8:16] + value_t[16:24]).astype(BF16).astype(F32)
    g_2.relay()
    lax.fori_loop(0, early * blocks, attend, 0)
    g_2.settle()
    links.drain()
    links.open = []
    lax.fori_loop(early, heads, project_late, 0)
    lax.fori_loop(early * blocks, heads * blocks, attend, 0)
    total = pv[0]
    for head in range(1, heads):
        total = total + pv[head]
    logit_s[...] = jnp.transpose(total)[0:8]
    tiny = [links.send(logit_s, logit_r.at[i], **step) for i, step in enumerate(CLIP_ALL)]
    dv_t[...] = jnp.zeros_like(dv_t)
    for copy in tiny:
        copy.wait_recv()
    logit = logit_s[...] + logit_r[0] + logit_r[1] + logit_r[2]
    soft = jnp.maximum(-logit, 0.0) + jnp.log1p(jnp.exp(-jnp.abs(logit)))
    loss = jnp.sum(soft, axis=1, keepdims=True) * (1.0 / tokens)
    lane = lax.broadcasted_iota(jnp.int32, (8, 128), 1)
    loss_mid[0] = jnp.where(lane == dp, jnp.broadcast_to(loss, (8, 128)), 0.0)

    def loss_step(index, axis):
        return [
            links.send(loss_mid.at[index], loss_buf.at[index, step - 1], **{axis: step})
            for step in (1, 2, 3)
        ]

    def loss_sum(index, copies):
        for copy in copies:
            copy.wait_recv()
        return loss_mid[index] + loss_buf[index, 0] + loss_buf[index, 1] + loss_buf[index, 2]

    tiny = loss_step(0, "y")
    dlog[...] = lanes_of((-1.0 / tokens) / (1.0 + jnp.exp(logit)), tokens)

    def backward(head, carry):
        def rows_of(index, d_value):
            rows = pl.ds(pl.multiple_of(index * block, block), block)
            weights = probs[head, rows]
            slope = dlog[rows][:, 0:1]
            tilt = vrow[pl.ds(head, 1)] - pv[head, rows][:, 0:1]
            d_sc[rows] = (weights * tilt * (slope * scale_dot)).astype(BF16)
            return d_value + jnp.sum(weights * slope, axis=0, keepdims=True)

        d_value = lax.fori_loop(0, blocks, rows_of, jnp.zeros((1, tokens), F32))
        d_value = d_value.astype(BF16).astype(F32)
        for term in range(3):
            dv_t[pl.ds(term * 8 + head, 1)] = d_value
        key = qk[:, pl.ds(pl.multiple_of(head * 256 + 128, 128), 128)]
        cosine, sine = tables[0], tables[1]
        d_query = dot(d_sc[...], key)
        d_key = jnp.transpose(dot(q_t[head], d_sc[...])).astype(BF16).astype(F32)
        d_query = d_query * cosine - pltpu.roll(d_query, 64, 1) * sine
        d_key = d_key * cosine - pltpu.roll(d_key, 64, 1) * sine
        start = head * 256 + ((head + early) // (2 * early)) * 128
        dqk[:, pl.ds(pl.multiple_of(start, 128), 128)] = d_query.astype(BF16)
        dqk[:, pl.ds(pl.multiple_of(start + 128, 128), 128)] = d_key.astype(BF16)
        return carry

    lax.fori_loop(0, heads, backward, 0)
    dqk[:, fold_at:late_at] = jnp.transpose(dv_t[...]).astype(BF16)
    loss_mid[1] = loss_sum(0, tiny)
    tiny = loss_step(1, "x")

    sums[...] = jnp.zeros_like(sums)

    def d_block(owner, rows):
        value = dot_t(dqk[rows, :late_at], wx_1_all[owner].reshape(cols, late_at))
        value = value + dot_t(dqk[rows, late_at:], wx_2_all[owner].reshape(cols, -1))
        normed = (tin[rows, col(owner)].astype(F32) - mean_c[rows][:, 0:1]) * inv_c[rows][:, 0:1]
        sums[0, rows] = sums[0, rows] + jnp.sum(value, axis=1, keepdims=True)
        sums[1, rows] = sums[1, rows] + jnp.sum(value * normed, axis=1, keepdims=True)
        return value

    pieces = [pl.ds(index * size, size) for index in range(2)]
    first, second, third = [], [], []
    for rows in pieces:
        stage[1, rows] = d_block(far_beside, rows).astype(BF16)
        first.append(links.send(stage.at[1, rows], from_core.at[1, rows], core=1))
    for index, rows in enumerate(pieces):
        value = d_block(far, rows)
        first[index].wait_recv()
        cross[rows] = (value + from_core[1, rows].astype(F32)).astype(BF16)
        second.append(links.send(cross.at[rows], from_chip.at[rows], zl=1))
    for rows in pieces:
        stage[0, rows] = d_block(beside_me, rows).astype(BF16)
        third.append(links.send(stage.at[0, rows], from_core.at[0, rows], core=1))
    for rows in pieces:
        own[rows] = d_block(me, rows)
    loss_mid[2] = loss_sum(1, tiny)
    tiny = loss_step(2, "zh")
    stats_s[0:8] = jnp.transpose(sums[0])[0:8]
    stats_s[8:16] = jnp.transpose(sums[1])[0:8]
    stats = [links.send(stats_s, stats_r.at[i], **step) for i, step in enumerate(CLIP_ALL)]
    for copy in stats:
        copy.wait_recv()
    both = (stats_s[...] + stats_r[0] + stats_r[1] + stats_r[2]) * (1.0 / channels)
    sums[0] = lanes_of(both[0:8], tokens)
    sums[1] = lanes_of(both[8:16], tokens)
    for index, rows in enumerate(pieces):
        third[index].wait_recv()
        second[index].wait_recv()
        value = own[rows] + from_core[0, rows].astype(F32) + from_chip[rows].astype(F32)
        inverse = inv_c[rows][:, 0:1]
        normed = (tin[rows, col(me)].astype(F32) - mean_c[rows][:, 0:1]) * inverse
        value = inverse * (value - sums[0, rows][:, 0:1] - normed * sums[1, rows][:, 0:1])
        dbr[rows] = (gate * keep * value).astype(BF16)

    grads = ws_all
    spare = list(bufs)
    stages = []
    for first_axis, second_axis, base in (("y", "x", 0), ("x", "y", 2)):
        big, spare = spare[:6], spare[6:]
        small, spare = spare[:6], spare[6:]
        mid, mid_b, spare = spare[0], spare[1], spare[2:]

        def plain1(half, step, axis=first_axis, other=second_axis, base=base):
            return grads.at[slot_of(links, axis, step, other, base + half)]

        def read1(half, step, plain=plain1):
            return plain(half, step)[...].astype(F32)

        def spot_of(step, axis=second_axis):
            return ({"x": links.x, "y": links.y}[axis] + step) % 4

        def plain2(half, step, mid_b=mid_b, spot=spot_of):
            return mid_b.at[half, spot(step)]

        def read2(half, step, mid=mid, spot=spot_of):
            return mid[half, spot(step)]

        stages.append(
            (
                base,
                mid,
                mid_b,
                Scatter(links, first_axis, read1, plain1, big),
                Scatter(links, second_axis, read2, plain2, small),
            )
        )
    for quarter in (0, 2, 1, 3):
        here = pl.ds(quarter * cols, cols)
        value = dot(mod_t[here], dbr[...]).astype(BF16)
        grads[quarter] = value.reshape(grads.shape[1:])
        stages[quarter // 2][3].start(quarter % 2)
    for pair in stages:
        pair[3].middle()
    for base, mid, mid_b, first_ring, second_ring in stages:

        def store(half, value, mid=mid, mid_b=mid_b):
            mid[half] = value
            mid_b[half] = value.astype(BF16)

        first_ring.finish(store)
        second_ring.start(0)
        second_ring.start(1)
    for pair in stages:
        pair[4].middle()
    for base, mid, mid_b, first_ring, second_ring in stages:

        def hold(half, value, base=base):
            z_keep[base + half] = value
            z_send[base + half] = value.astype(BF16)

        second_ring.finish(hold)
    tail = [
        links.send(z_send.at[(links.zh + step) % 4], z_recv.at[step - 1], zh=step)
        for step in (1, 3, 2)
    ]
    loss_o[...] = loss_sum(2, tiny)
    for copy in tail:
        copy.wait_recv()
    grad_o[...] = (
        z_keep[links.zh]
        + z_recv[0].astype(F32)
        + z_recv[1].astype(F32)
        + z_recv[2].astype(F32)
    )
    links.drain()


def shards(latents, noise, steps, layout, w_time, w_student, w_qk, w_value, w_disc):
    channels = latents.shape[1]
    tokens, cols = noise.shape
    rows = w_student.shape[0]
    heads = cols // HD
    wide = w_qk.shape[1] + 128
    narrow = (heads - 1) // 2 * 2 * HD + 128
    big = [VMEM((4, rows, cols), BF16)] * 4 + [VMEM((2, 4, rows, cols), BF16)] * 2
    small = [VMEM((rows, cols), BF16)] * 4 + [VMEM((2, rows, cols), BF16)] * 2
    mids = [VMEM((2, 4, rows, cols), F32), VMEM((2, 4, rows, cols), BF16)]
    scratch = [
        pltpu.SemaphoreType.DMA((128,)),
        pltpu.SemaphoreType.DMA((128,)),
        pltpu.SemaphoreType.DMA((5,)),
        VMEM(w_time.shape, BF16),
        VMEM((rows, narrow), BF16),
        VMEM((rows, wide - narrow), BF16),
        VMEM((4, 4, 4, rows, cols), BF16),
        VMEM((4, 4, 4, rows, narrow), BF16),
        VMEM((4, 4, 4, rows, wide - narrow), BF16),
        VMEM((4,) + latents.shape, BF16),
        VMEM((8, w_time.shape[1]), F32),
        VMEM((tokens, channels), BF16),
        VMEM((channels, tokens), BF16),
        VMEM((tokens, cols), BF16),
        VMEM((tokens, channels), BF16),
        VMEM((tokens, 128), F32),
        VMEM((tokens, 128), F32),
        VMEM((2, tokens, 128), F32),
        VMEM((tokens, 2 * cols), BF16),
        VMEM((heads, HD, tokens), BF16),
        VMEM((heads, tokens, tokens), F32),
        VMEM((heads, tokens, 128), F32),
        VMEM((8, tokens), F32),
        VMEM((8, tokens), F32),
        VMEM((3, 8, tokens), F32),
        VMEM((tokens, 128), F32),
        VMEM((tokens, tokens), BF16),
        VMEM((128, tokens), F32),
        VMEM((tokens, wide), BF16),
        VMEM((2, tokens, cols), BF16),
        VMEM((2, tokens, cols), BF16),
        VMEM((tokens, cols), BF16),
        VMEM((tokens, cols), BF16),
        VMEM((tokens, cols), F32),
        VMEM((2, tokens, 128), F32),
        VMEM((16, tokens), F32),
        VMEM((3, 16, tokens), F32),
        VMEM((tokens, cols), BF16),
        VMEM((3, 3, 8, 128), F32),
        VMEM((3, 8, 128), F32),
        VMEM((4, rows, cols), BF16),
        VMEM((3, rows, cols), BF16),
        VMEM((4, rows, cols), F32),
    ] + (big + small + mids) * 2
    student_grad, losses = pl.pallas_call(
        step_body,
        out_shape=(
            jax.ShapeDtypeStruct((rows, cols), F32),
            jax.ShapeDtypeStruct((8, 128), F32),
        ),
        in_specs=[
            VSPEC,
            VSPEC,
            pl.BlockSpec(memory_space=pltpu.SMEM),
            VSPEC,
            ASPEC,
            VSPEC,
            VSPEC,
            VSPEC,
            VSPEC,
        ],
        out_specs=(VSPEC, VSPEC),
        scratch_shapes=scratch,
        compiler_params=pltpu.CompilerParams(
            collective_id=1, has_side_effects=True, vmem_limit_bytes=67043328
        ),
    )(latents, noise, steps, layout, w_time, w_student, w_qk, w_value, w_disc.reshape(1, cols))
    return (losses[0, : steps.shape[0]], student_grad)


def solution(mesh):
    return jax.shard_map(
        shards,
        mesh=mesh,
        in_specs=(
            P(("dp", "ctx"), None),
            P("dp", "ctx"),
            P(),
            P("dp", None),
            P(),
            P("dp", "ctx"),
            P("dp", "ctx"),
            P("dp", "ctx"),
            P("ctx"),
        ),
        out_specs=(P(), P("dp", "ctx")),
        check_vma=False,
    )
```

```python
import functools
import math

import jax
import jax.numpy as jnp
from jax import lax
from jax.experimental import pallas as pl
from jax.experimental.pallas import tpu as pltpu
from jax.sharding import PartitionSpec as P

HD = 128
FREQ = 256
STEPS = 1000
MESH = pl.DeviceIdType.MESH
VMEM = pltpu.VMEM
VSPEC = pl.BlockSpec(memory_space=pltpu.VMEM)
ASPEC = pl.BlockSpec(memory_space=pl.ANY)
F32 = jnp.float32
BF16 = jnp.bfloat16


ln_eps = 1e-06
exact_dots = lax.Precision.HIGHEST


def place():
    d = lax.axis_index("dp")
    c = lax.axis_index("ctx")
    return d // 16, (d // 4) % 4, d % 4, c // 2, c % 2


class Links:
    def __init__(self, send_sems, recv_sems):
        self.send_sems, self.recv_sems = send_sems, recv_sems
        self.used = 0
        self.open = []
        self.zh, self.x, self.y, self.zl, self.core = place()

    def dev(self, zh=0, x=0, y=0, zl=0, core=0):
        z_new = (self.zh + zh) % 4
        x_new = (self.x + x) % 4
        y_new = (self.y + y) % 4
        return (
            z_new * 16 + x_new * 4 + y_new,
            ((self.zl + zl) % 2) * 2 + (self.core + core) % 2,
        )

    def barrier(self, steps):
        sem = pltpu.get_barrier_semaphore()
        for step in steps:
            pl.semaphore_signal(sem, inc=1, device_id=self.dev(**step), device_id_type=MESH)
        pl.semaphore_wait(sem, len(steps))

    def send(self, src, dst, **step):
        slot = self.used
        self.used += 1
        copy = pltpu.make_async_remote_copy(
            src_ref=src,
            dst_ref=dst,
            send_sem=self.send_sems.at[slot],
            recv_sem=self.recv_sems.at[slot],
            device_id=self.dev(**step),
            device_id_type=MESH,
        )
        copy.start()
        self.open.append(copy)
        return copy

    def drain(self):
        for copy in self.open:
            copy.wait_send()


AXES_AB = (("x", "y", 0), ("y", "x", 2))


def slot_of(links, axis, step, other=None, zs=slice(0, 2)):
    moved = {"x": links.x, "y": links.y}
    moved[axis] = (moved[axis] + step) % 4
    picks = dict(moved)
    if other is not None:
        picks[other] = slice(None)
    return (zs, picks["x"], picks["y"])


class Gather:
    def __init__(self, links, shard, out, loc_sem):
        self.links, self.shard, self.out = links, shard, out
        self.own = pltpu.make_async_copy(shard, out.at[links.zh, links.x, links.y], loc_sem)

    def along_z(self):
        links = self.links
        self.own.start()
        home = self.out.at[links.zh, links.x, links.y]
        self.copies = [links.send(self.shard, home, zh=step) for step in (1, 3, 2)]

    def settle(self):
        for copy in self.copies:
            copy.wait_recv()
        self.copies = []

    def spread(self, second):
        links = self.links
        if not second:
            self.own.wait()
        self.settle()
        self.near = []
        for first_axis, second_axis, base in AXES_AB:
            axis = second_axis if second else first_axis
            other = first_axis if second else None
            mine = self.out.at[slot_of(links, axis, 0, other, slice(base, base + 2))]
            self.near.append(
                (
                    axis,
                    other,
                    base,
                    links.send(mine, mine, **{axis: 1}),
                    links.send(mine, mine, **{axis: 3}),
                )
            )

    def relay(self):
        links = self.links
        self.copies = []
        for axis, other, base, up, down in self.near:
            up.wait_recv()
            piece = self.out.at[slot_of(links, axis, 3, other, base)]
            self.copies.append(links.send(piece, piece, **{axis: 1}))
            down.wait_recv()
            piece = self.out.at[slot_of(links, axis, 1, other, base + 1)]
            self.copies.append(links.send(piece, piece, **{axis: 3}))


NEAR = (
    dict(core=1),
    dict(zl=1),
    dict(zl=1, core=1),
    dict(zh=1),
    dict(zh=2),
    dict(zh=3),
    dict(x=1),
    dict(x=2),
    dict(x=3),
    dict(y=1),
    dict(y=2),
    dict(y=3),
)
CLIP_ALL = NEAR[:3]


class Scatter:
    def __init__(self, links, axis, read, plain, bufs):
        self.links, self.axis, self.read, self.plain = links, axis, read, plain
        self.one_up, self.one_down, self.mix_up, self.mix_down, self.two_up, self.two_down = bufs
        self.last = []

    def start(self, half):
        links, axis, plain = self.links, self.axis, self.plain
        if half == 0:
            self.up = links.send(plain(0, 2), self.one_up, **{axis: 1})
            self.last.append(links.send(plain(0, 3), self.two_down.at[0], **{axis: 3}))
        else:
            self.down = links.send(plain(1, 2), self.one_down, **{axis: 3})
            self.last.append(links.send(plain(1, 1), self.two_up.at[1], **{axis: 1}))

    def middle(self):
        links, axis = self.links, self.axis
        self.up.wait_recv()
        self.mix_up[...] = (self.read(0, 1) + self.one_up[...].astype(F32)).astype(BF16)
        self.last.append(links.send(self.mix_up, self.two_up.at[0], **{axis: 1}))
        self.down.wait_recv()
        self.mix_down[...] = (self.read(1, 3) + self.one_down[...].astype(F32)).astype(BF16)
        self.last.append(links.send(self.mix_down, self.two_down.at[1], **{axis: 3}))

    def finish(self, store):
        for copy in self.last:
            copy.wait_recv()
        for half in range(2):
            store(
                half,
                self.read(half, 0)
                + self.two_up[half].astype(F32)
                + self.two_down[half].astype(F32),
            )


class Direct:
    def __init__(self, links, axis, read, plain, inbox):
        self.links, self.axis, self.read, self.plain, self.inbox = links, axis, read, plain, inbox

    def start(self):
        self.copies = [
            self.links.send(self.plain(step), self.inbox.at[step - 1], **{self.axis: step})
            for step in (1, 3, 2)
        ]

    def finish(self, store):
        for copy in self.copies:
            copy.wait_recv()
        for half in range(2):
            value = self.read(half)
            for index in range(3):
                value = value + self.inbox[index, half].astype(F32)
            store(half, value)


def dot(a, b):
    return jnp.dot(a, b, preferred_element_type=F32)


def dot_t(a, b):
    return lax.dot_general(a, b, (((1,), (1,)), ((), ())), preferred_element_type=F32)


def lanes_of(row, count):
    return jnp.transpose(jnp.broadcast_to(row[0:1], (128, count)))


def step_body(
    lat, noise, steps, layout, w_time, ws, wqk, wv, disc,
    grad_o, loss_o,
    send_sems, recv_sems, loc_sems,
    wt, wx_1, wx_2, ws_all, wx_1_all, wx_2_all, lat_all, mod, modin, mod_t, part, tin, mean_c, inv_c,
    tables, qk, q_t, probs, pv, vrow, logit_s, logit_r, dlog, d_sc, dv_t, dqk,
    stage, from_core, cross, from_chip, own, sums, stats_s, stats_r, dbr,
    loss_buf, loss_mid, z_send, z_recv, z_keep, *bufs,
):
    links = Links(send_sems, recv_sems)
    tokens, cols = noise.shape
    channels = lat.shape[1]
    rows_each = lat.shape[0]
    heads = cols // HD
    dp, zl, core = lax.axis_index("dp"), links.zl, links.core
    me = zl * 2 + core
    beside_me = zl * 2 + (core + 1) % 2
    far = ((zl + 1) % 2) * 2 + core
    far_beside = ((zl + 1) % 2) * 2 + (core + 1) % 2
    early = (heads - 1) // 2
    fold_at = early * 2 * HD
    late_at = fold_at + 128

    def col(owner, base=0):
        return pl.ds(pl.multiple_of(base + owner * cols, 128), cols)

    get_wt = pltpu.make_async_copy(w_time, wt, loc_sems.at[0])
    get_wt.start()
    links.barrier(NEAR)
    g_ws = Gather(links, ws, ws_all, loc_sems.at[1])
    g_1 = Gather(links, wx_1, wx_1_all, loc_sems.at[2])
    g_2 = Gather(links, wx_2, wx_2_all, loc_sems.at[4])
    g_ws.along_z()

    lane = lax.broadcasted_iota(jnp.int32, (ws.shape[0], 128), 1)
    scaled = wv[...].astype(F32) * disc[...].reshape(1, cols)
    extra = jnp.zeros((ws.shape[0], 128), F32)
    for head in range(heads):
        value = jnp.sum(scaled[:, head * HD : (head + 1) * HD], axis=1, keepdims=True)
        for term in range(3):
            piece = value.astype(BF16).astype(F32)
            extra = jnp.where(lane == term * 8 + head, piece, extra)
            value = value - piece
    wx_1[:, :fold_at] = wqk[:, :fold_at]
    wx_1[:, fold_at:] = extra.astype(BF16)
    wx_2[...] = wqk[:, fold_at:]
    g_1.along_z()
    own_lat = pltpu.make_async_copy(lat, lat_all.at[me], loc_sems.at[3])
    own_lat.start()
    halves = [slice(0, rows_each // 2), slice(rows_each // 2, rows_each)]
    across = [links.send(lat.at[h], lat_all.at[me, h], zl=1) for h in halves]
    beside = links.send(lat, lat_all.at[me], core=1)
    g_2.along_z()

    step_f = jnp.full((8, 128), steps[dp], jnp.int32).astype(F32)
    spot = lax.broadcasted_iota(jnp.int32, (8, 128), 1).astype(F32)
    angle = step_f * jnp.exp(-math.log(10000.0) * spot / (FREQ // 2))
    embed = jnp.concatenate([jnp.cos(angle), jnp.sin(angle)], axis=1).astype(BF16)
    sigma = (0.25 + 0.5 * step_f / STEPS)[0:1, 0:1]
    get_wt.wait()
    for third in range(3):
        here = slice(third * channels, (third + 1) * channels)
        mod[:, here] = dot(embed, wt[:, here])
    g_ws.spread(False)

    def norm_rows(owner):
        def rows16(index, carry):
            rows = pl.ds(pl.multiple_of(index * 16, 16), 16)
            value = lat_all[owner, rows].astype(F32)
            value = value - jnp.sum(value, axis=1, keepdims=True) * (1.0 / channels)
            spread = jnp.sum(value * value, axis=1, keepdims=True) * (1.0 / channels)
            value = value * lax.rsqrt(spread + ln_eps)
            value = value * (1.0 + mod[0:1, channels : 2 * channels]) + mod[0:1, :channels]
            modin[pl.ds(pl.multiple_of(owner * rows_each + index * 16, 16), 16)] = value.astype(BF16)
            return carry

        lax.fori_loop(0, rows_each // 16, rows16, 0)

    own_lat.wait()
    norm_rows(me)
    g_ws.relay()
    g_1.spread(False)
    beside.wait_recv()
    norm_rows(beside_me)
    g_ws.spread(True)
    g_1.relay()

    place_c = lanes_of(layout[...].astype(F32), tokens)
    lane = lax.broadcasted_iota(jnp.int32, (tokens, 128), 1)
    omega = jnp.exp(-math.log(10000.0) * (lane % 64).astype(F32) / 64)
    tables[0] = jnp.cos(place_c * omega)
    sine = jnp.sin(place_c * omega)
    tables[1] = jnp.where(lane < 64, -sine, sine)

    g_ws.relay()
    g_1.spread(True)
    passed = []
    for copy, h in zip(across, halves):
        copy.wait_recv()
        passed.append(links.send(lat_all.at[far, h], lat_all.at[far, h], core=1))
    norm_rows(far)
    g_2.spread(False)
    for copy in passed:
        copy.wait_recv()
    norm_rows(far_beside)

    def flip(index, carry):
        here = pl.ds(pl.multiple_of(index * 128, 128), 128)
        mod_t[here] = jnp.transpose(modin[:, here].astype(F32)).astype(BF16)
        return carry

    g_ws.settle()
    gate = mod[0:1, col(me, 2 * channels)]
    keep = 1.0 - sigma
    size = tokens // 2
    sent, near = [], []
    for index in range(2):
        rows = pl.ds(index * size, size)
        branch = dot(modin[rows], ws_all[...].reshape(channels, cols))
        mine = lat_all[pl.ds(index * 2, 2), :, col(me)].reshape(size, cols).astype(F32)
        mixed = keep * (mine + gate * branch) + sigma * noise[rows].astype(F32)
        part[rows] = mixed.astype(BF16)
        sent.append(links.send(part.at[rows], tin.at[rows, col(me)], zl=1))
        near.append(links.send(part.at[rows], tin.at[rows, col(me)], core=1))
        tin[rows, col(me)] = mixed.astype(BF16)
    g_1.relay()
    g_2.relay()
    g_2.spread(True)
    lax.fori_loop(0, channels // 128, flip, 0)

    passed = []
    for index in range(2):
        rows = pl.ds(index * size, size)
        sent[index].wait_recv()
        passed.append(links.send(tin.at[rows, col(far)], tin.at[rows, col(far)], core=1))
    tnorm_b = modin
    for index in range(2):
        near[index].wait_recv()
        passed[index].wait_recv()

        def rows16(step, carry):
            rows = pl.ds(pl.multiple_of(index * size + step * 16, 16), 16)
            value = tin[rows].astype(F32)
            mean = jnp.sum(value, axis=1, keepdims=True) * (1.0 / channels)
            value = value - mean
            spread = jnp.sum(value * value, axis=1, keepdims=True) * (1.0 / channels)
            inverse = lax.rsqrt(spread + ln_eps)
            tnorm_b[rows] = (value * inverse).astype(BF16)
            mean_c[rows] = jnp.broadcast_to(mean, (16, 128))
            inv_c[rows] = jnp.broadcast_to(inverse, (16, 128))
            return carry

        lax.fori_loop(0, size // 16, rows16, 0)
        if index == 0:
            g_2.relay()
    g_1.settle()

    def project(head, source, base):
        weights = source[:, :, :, :, pl.ds(pl.multiple_of(head * 256 - base, 256), 256)]
        both = dot(tnorm_b[...], weights.reshape(channels, 256))
        cosine, sine = tables[0], tables[1]
        query, key = both[:, :HD], both[:, HD:]
        query = query * cosine + pltpu.roll(query, 64, 1) * sine
        key = key * cosine + pltpu.roll(key, 64, 1) * sine
        qk[:, pl.ds(pl.multiple_of(head * 256, 256), 128)] = query.astype(BF16)
        qk[:, pl.ds(pl.multiple_of(head * 256 + 128, 128), 128)] = key.astype(BF16)
        q_t[head] = jnp.transpose(query).astype(BF16)

    scale_dot = 1.0 / math.sqrt(HD)
    block = 128
    blocks = tokens // block

    def attend(trip, carry):
        head, index = trip // blocks, trip % blocks
        rows = pl.ds(pl.multiple_of(index * block, block), block)
        query = qk[rows, pl.ds(pl.multiple_of(head * 256, 256), 128)]
        key = qk[:, pl.ds(pl.multiple_of(head * 256 + 128, 128), 128)]
        scores = dot_t(query, key) * scale_dot
        weights = jnp.exp(scores - jnp.max(scores, axis=1, keepdims=True))
        weights = weights * (1.0 / jnp.sum(weights, axis=1, keepdims=True))
        probs[head, rows] = weights
        share = jnp.sum(weights * vrow[pl.ds(head, 1)], axis=1, keepdims=True)
        pv[head, rows] = jnp.broadcast_to(share, (block, 128))
        return carry

    def project_early(head, carry):
        project(head, wx_1_all, 0)
        return carry

    def project_late(head, carry):
        project(head, wx_2_all, fold_at)
        return carry

    lax.fori_loop(0, early, project_early, 0)
    value_t = jnp.transpose(
        dot(tnorm_b[...], wx_1_all[:, :, :, :, pl.ds(fold_at, 128)].reshape(channels, 128))
    )
    vrow[...] = (value_t[0:8] + value_t[8:16] + value_t[16:24]).astype(BF16).astype(F32)
    lax.fori_loop(0, early * blocks, attend, 0)
    g_2.settle()
    links.drain()
    links.open = []
    lax.fori_loop(early, heads, project_late, 0)
    lax.fori_loop(early * blocks, heads * blocks, attend, 0)
    total = pv[0]
    for head in range(1, heads):
        total = total + pv[head]
    logit_s[...] = jnp.transpose(total)[0:8]
    tiny = [links.send(logit_s, logit_r.at[i], **step) for i, step in enumerate(CLIP_ALL)]
    dv_t[...] = jnp.zeros_like(dv_t)
    for copy in tiny:
        copy.wait_recv()
    logit = logit_s[...] + logit_r[0] + logit_r[1] + logit_r[2]
    soft = jnp.maximum(-logit, 0.0) + jnp.log1p(jnp.exp(-jnp.abs(logit)))
    loss = jnp.sum(soft, axis=1, keepdims=True) * (1.0 / tokens)
    lane = lax.broadcasted_iota(jnp.int32, (8, 128), 1)
    loss_mid[0] = jnp.where(lane == dp, jnp.broadcast_to(loss, (8, 128)), 0.0)

    def loss_step(index, axis):
        return [
            links.send(loss_mid.at[index], loss_buf.at[index, step - 1], **{axis: step})
            for step in (1, 2, 3)
        ]

    def loss_sum(index, copies):
        for copy in copies:
            copy.wait_recv()
        return loss_mid[index] + loss_buf[index, 0] + loss_buf[index, 1] + loss_buf[index, 2]

    tiny = loss_step(0, "y")
    dlog[...] = lanes_of((-1.0 / tokens) / (1.0 + jnp.exp(logit)), tokens)

    def backward(head, carry):
        def rows_of(index, d_value):
            rows = pl.ds(pl.multiple_of(index * block, block), block)
            weights = probs[head, rows]
            slope = dlog[rows][:, 0:1]
            tilt = vrow[pl.ds(head, 1)] - pv[head, rows][:, 0:1]
            d_sc[rows] = (weights * tilt * (slope * scale_dot)).astype(BF16)
            return d_value + jnp.sum(weights * slope, axis=0, keepdims=True)

        d_value = lax.fori_loop(0, blocks, rows_of, jnp.zeros((1, tokens), F32))
        d_value = d_value.astype(BF16).astype(F32)
        for term in range(3):
            dv_t[pl.ds(term * 8 + head, 1)] = d_value
        key = qk[:, pl.ds(pl.multiple_of(head * 256 + 128, 128), 128)]
        cosine, sine = tables[0], tables[1]
        d_query = dot(d_sc[...], key)
        d_key = jnp.transpose(dot(q_t[head], d_sc[...])).astype(BF16).astype(F32)
        d_query = d_query * cosine - pltpu.roll(d_query, 64, 1) * sine
        d_key = d_key * cosine - pltpu.roll(d_key, 64, 1) * sine
        start = head * 256 + ((head + early) // (2 * early)) * 128
        dqk[:, pl.ds(pl.multiple_of(start, 128), 128)] = d_query.astype(BF16)
        dqk[:, pl.ds(pl.multiple_of(start + 128, 128), 128)] = d_key.astype(BF16)
        return carry

    lax.fori_loop(0, heads, backward, 0)
    dqk[:, fold_at:late_at] = jnp.transpose(dv_t[...]).astype(BF16)
    loss_mid[1] = loss_sum(0, tiny)
    tiny = loss_step(1, "x")

    sums[...] = jnp.zeros_like(sums)

    def d_block(owner, rows):
        value = dot_t(dqk[rows, :late_at], wx_1_all[owner].reshape(cols, late_at))
        value = value + dot_t(dqk[rows, late_at:], wx_2_all[owner].reshape(cols, -1))
        normed = (tin[rows, col(owner)].astype(F32) - mean_c[rows][:, 0:1]) * inv_c[rows][:, 0:1]
        sums[0, rows] = sums[0, rows] + jnp.sum(value, axis=1, keepdims=True)
        sums[1, rows] = sums[1, rows] + jnp.sum(value * normed, axis=1, keepdims=True)
        return value

    pieces = [pl.ds(index * size, size) for index in range(2)]
    first, second, third = [], [], []
    for rows in pieces:
        stage[1, rows] = d_block(far_beside, rows).astype(BF16)
        first.append(links.send(stage.at[1, rows], from_core.at[1, rows], core=1))
    for index, rows in enumerate(pieces):
        value = d_block(far, rows)
        first[index].wait_recv()
        cross[rows] = (value + from_core[1, rows].astype(F32)).astype(BF16)
        second.append(links.send(cross.at[rows], from_chip.at[rows], zl=1))
    for rows in pieces:
        stage[0, rows] = d_block(beside_me, rows).astype(BF16)
        third.append(links.send(stage.at[0, rows], from_core.at[0, rows], core=1))
    for rows in pieces:
        own[rows] = d_block(me, rows)
    loss_mid[2] = loss_sum(1, tiny)
    tiny = loss_step(2, "zh")
    stats_s[0:8] = jnp.transpose(sums[0])[0:8]
    stats_s[8:16] = jnp.transpose(sums[1])[0:8]
    stats = [links.send(stats_s, stats_r.at[i], **step) for i, step in enumerate(CLIP_ALL)]
    for copy in stats:
        copy.wait_recv()
    both = (stats_s[...] + stats_r[0] + stats_r[1] + stats_r[2]) * (1.0 / channels)
    sums[0] = lanes_of(both[0:8], tokens)
    sums[1] = lanes_of(both[8:16], tokens)
    for index, rows in enumerate(pieces):
        third[index].wait_recv()
        second[index].wait_recv()
        value = own[rows] + from_core[0, rows].astype(F32) + from_chip[rows].astype(F32)
        inverse = inv_c[rows][:, 0:1]
        normed = (tin[rows, col(me)].astype(F32) - mean_c[rows][:, 0:1]) * inverse
        value = inverse * (value - sums[0, rows][:, 0:1] - normed * sums[1, rows][:, 0:1])
        dbr[rows] = (gate * keep * value).astype(BF16)

    grads = ws_all
    spare = list(bufs)
    stages = []
    for first_axis, second_axis, base in (("y", "x", 0), ("x", "y", 2)):
        big, spare = spare[:6], spare[6:]
        inbox, mid, mid_b = spare[:3]
        spare = spare[3:]

        def plain1(half, step, axis=first_axis, other=second_axis, base=base):
            return grads.at[slot_of(links, axis, step, other, base + half)]

        def read1(half, step, plain=plain1):
            return plain(half, step)[...].astype(F32)

        def spot_of(step, axis=second_axis):
            return ({"x": links.x, "y": links.y}[axis] + step) % 4

        def plain2(step, mid_b=mid_b, spot=spot_of):
            return mid_b.at[:, spot(step)]

        def read2(half, mid=mid, spot=spot_of):
            return mid[half, spot(0)]

        stages.append(
            (
                base,
                mid,
                mid_b,
                Scatter(links, first_axis, read1, plain1, big),
                Direct(links, second_axis, read2, plain2, inbox),
            )
        )
    for quarter in (0, 2, 1, 3):
        here = pl.ds(quarter * cols, cols)
        value = dot(mod_t[here], dbr[...]).astype(BF16)
        grads[quarter] = value.reshape(grads.shape[1:])
        stages[quarter // 2][3].start(quarter % 2)
    for pair in stages:
        pair[3].middle()
    for base, mid, mid_b, first_ring, second_ring in stages:

        def store(half, value, mid=mid, mid_b=mid_b):
            mid[half] = value
            mid_b[half] = value.astype(BF16)

        first_ring.finish(store)
        second_ring.start()
    for base, mid, mid_b, first_ring, second_ring in stages:

        def hold(half, value, base=base):
            z_keep[base + half] = value
            z_send[base + half] = value.astype(BF16)

        second_ring.finish(hold)
    tail = [
        links.send(z_send.at[(links.zh + step) % 4], z_recv.at[step - 1], zh=step)
        for step in (1, 3, 2)
    ]
    loss_o[...] = loss_sum(2, tiny)
    for copy in tail:
        copy.wait_recv()
    grad_o[...] = (
        z_keep[links.zh]
        + z_recv[0].astype(F32)
        + z_recv[1].astype(F32)
        + z_recv[2].astype(F32)
    )
    links.drain()


def shards(latents, noise, steps, layout, w_time, w_student, w_qk, w_value, w_disc):
    channels = latents.shape[1]
    tokens, cols = noise.shape
    rows = w_student.shape[0]
    heads = cols // HD
    wide = w_qk.shape[1] + 128
    narrow = (heads - 1) // 2 * 2 * HD + 128
    big = [VMEM((4, rows, cols), BF16)] * 4 + [VMEM((2, 4, rows, cols), BF16)] * 2
    small = [VMEM((3, 2, rows, cols), BF16)]
    mids = [VMEM((2, 4, rows, cols), F32), VMEM((2, 4, rows, cols), BF16)]
    scratch = [
        pltpu.SemaphoreType.DMA((128,)),
        pltpu.SemaphoreType.DMA((128,)),
        pltpu.SemaphoreType.DMA((5,)),
        VMEM(w_time.shape, BF16),
        VMEM((rows, narrow), BF16),
        VMEM((rows, wide - narrow), BF16),
        VMEM((4, 4, 4, rows, cols), BF16),
        VMEM((4, 4, 4, rows, narrow), BF16),
        VMEM((4, 4, 4, rows, wide - narrow), BF16),
        VMEM((4,) + latents.shape, BF16),
        VMEM((8, w_time.shape[1]), F32),
        VMEM((tokens, channels), BF16),
        VMEM((channels, tokens), BF16),
        VMEM((tokens, cols), BF16),
        VMEM((tokens, channels), BF16),
        VMEM((tokens, 128), F32),
        VMEM((tokens, 128), F32),
        VMEM((2, tokens, 128), F32),
        VMEM((tokens, 2 * cols), BF16),
        VMEM((heads, HD, tokens), BF16),
        VMEM((heads, tokens, tokens), F32),
        VMEM((heads, tokens, 128), F32),
        VMEM((8, tokens), F32),
        VMEM((8, tokens), F32),
        VMEM((3, 8, tokens), F32),
        VMEM((tokens, 128), F32),
        VMEM((tokens, tokens), BF16),
        VMEM((128, tokens), F32),
        VMEM((tokens, wide), BF16),
        VMEM((2, tokens, cols), BF16),
        VMEM((2, tokens, cols), BF16),
        VMEM((tokens, cols), BF16),
        VMEM((tokens, cols), BF16),
        VMEM((tokens, cols), F32),
        VMEM((2, tokens, 128), F32),
        VMEM((16, tokens), F32),
        VMEM((3, 16, tokens), F32),
        VMEM((tokens, cols), BF16),
        VMEM((3, 3, 8, 128), F32),
        VMEM((3, 8, 128), F32),
        VMEM((4, rows, cols), BF16),
        VMEM((3, rows, cols), BF16),
        VMEM((4, rows, cols), F32),
    ] + (big + small + mids) * 2
    student_grad, losses = pl.pallas_call(
        step_body,
        out_shape=(
            jax.ShapeDtypeStruct((rows, cols), F32),
            jax.ShapeDtypeStruct((8, 128), F32),
        ),
        in_specs=[
            VSPEC,
            VSPEC,
            pl.BlockSpec(memory_space=pltpu.SMEM),
            VSPEC,
            ASPEC,
            VSPEC,
            VSPEC,
            VSPEC,
            VSPEC,
        ],
        out_specs=(VSPEC, VSPEC),
        scratch_shapes=scratch,
        compiler_params=pltpu.CompilerParams(
            collective_id=1, has_side_effects=True, vmem_limit_bytes=67043328
        ),
    )(latents, noise, steps, layout, w_time, w_student, w_qk, w_value, w_disc)
    return (losses[0, : steps.shape[0]], student_grad)


def solution(mesh):
    return jax.shard_map(
        shards,
        mesh=mesh,
        in_specs=(
            P(("dp", "ctx"), None),
            P("dp", "ctx"),
            P(),
            P("dp", None),
            P(),
            P("dp", "ctx"),
            P("dp", "ctx"),
            P("dp", "ctx"),
            P("ctx"),
        ),
        out_specs=(P(), P("dp", "ctx")),
        check_vma=False,
    )
```

```python
import functools
import math

import jax
import jax.numpy as jnp
from jax import lax
from jax.experimental import pallas as pl
from jax.experimental.pallas import tpu as pltpu
from jax.sharding import PartitionSpec as P

HD = 128
FREQ = 256
STEPS = 1000
MESH = pl.DeviceIdType.MESH
VMEM = pltpu.VMEM
VSPEC = pl.BlockSpec(memory_space=pltpu.VMEM)
ASPEC = pl.BlockSpec(memory_space=pl.ANY)
F32 = jnp.float32
BF16 = jnp.bfloat16


ln_eps = 1e-06
exact_dots = lax.Precision.HIGHEST


def place():
    d = lax.axis_index("dp")
    c = lax.axis_index("ctx")
    return d // 16, (d // 4) % 4, d % 4, c // 2, c % 2


class Links:
    def __init__(self, send_sems, recv_sems):
        self.send_sems, self.recv_sems = send_sems, recv_sems
        self.used = 0
        self.open = []
        self.zh, self.x, self.y, self.zl, self.core = place()

    def dev(self, zh=0, x=0, y=0, zl=0, core=0):
        z_new = (self.zh + zh) % 4
        x_new = (self.x + x) % 4
        y_new = (self.y + y) % 4
        return (
            z_new * 16 + x_new * 4 + y_new,
            ((self.zl + zl) % 2) * 2 + (self.core + core) % 2,
        )

    def barrier(self, steps):
        sem = pltpu.get_barrier_semaphore()
        for step in steps:
            pl.semaphore_signal(sem, inc=1, device_id=self.dev(**step), device_id_type=MESH)
        pl.semaphore_wait(sem, len(steps))

    def send(self, src, dst, **step):
        slot = self.used
        self.used += 1
        copy = pltpu.make_async_remote_copy(
            src_ref=src,
            dst_ref=dst,
            send_sem=self.send_sems.at[slot],
            recv_sem=self.recv_sems.at[slot],
            device_id=self.dev(**step),
            device_id_type=MESH,
        )
        copy.start()
        self.open.append(copy)
        return copy

    def drain(self):
        for copy in self.open:
            copy.wait_send()


AXES_AB = (("x", "y", 0), ("y", "x", 2))


def slot_of(links, axis, step, other=None, zs=slice(0, 2)):
    moved = {"x": links.x, "y": links.y}
    moved[axis] = (moved[axis] + step) % 4
    picks = dict(moved)
    if other is not None:
        picks[other] = slice(None)
    return (zs, picks["x"], picks["y"])


class Gather:
    def __init__(self, links, shard, out, loc_sem):
        self.links, self.shard, self.out = links, shard, out
        self.own = pltpu.make_async_copy(shard, out.at[links.zh, links.x, links.y], loc_sem)

    def along_z(self):
        links = self.links
        self.own.start()
        home = self.out.at[links.zh, links.x, links.y]
        self.copies = [links.send(self.shard, home, zh=step) for step in (1, 3, 2)]

    def settle(self):
        for copy in self.copies:
            copy.wait_recv()
        self.copies = []

    def spread(self, second):
        links = self.links
        if not second:
            self.own.wait()
        self.settle()
        self.near = []
        for first_axis, second_axis, base in AXES_AB:
            axis = second_axis if second else first_axis
            other = first_axis if second else None
            half = [self.out.at[slot_of(links, axis, 0, other, base + i)] for i in range(2)]
            up = links.send(half[0], half[0], **{axis: 1})
            down = links.send(half[1], half[1], **{axis: 3})
            self.near.append((axis, other, base, up, down))
            self.copies.append(links.send(half[1], half[1], **{axis: 1}))
            self.copies.append(links.send(half[0], half[0], **{axis: 3}))

    def relay(self):
        links = self.links
        for axis, other, base, up, down in self.near:
            up.wait_recv()
            piece = self.out.at[slot_of(links, axis, 3, other, base)]
            self.copies.append(links.send(piece, piece, **{axis: 1}))
            down.wait_recv()
            piece = self.out.at[slot_of(links, axis, 1, other, base + 1)]
            self.copies.append(links.send(piece, piece, **{axis: 3}))


NEAR = (
    dict(core=1),
    dict(zl=1),
    dict(zl=1, core=1),
    dict(zh=1),
    dict(zh=2),
    dict(zh=3),
    dict(x=1),
    dict(x=2),
    dict(x=3),
    dict(y=1),
    dict(y=2),
    dict(y=3),
)
CLIP_ALL = NEAR[:3]


class Scatter:
    def __init__(self, links, axis, read, plain, bufs):
        self.links, self.axis, self.read, self.plain = links, axis, read, plain
        self.one_up, self.one_down, self.mix_up, self.mix_down, self.two_up, self.two_down = bufs
        self.last = []

    def start(self, half):
        links, axis, plain = self.links, self.axis, self.plain
        if half == 0:
            self.up = links.send(plain(0, 2), self.one_up, **{axis: 1})
            self.last.append(links.send(plain(0, 3), self.two_down.at[0], **{axis: 3}))
        else:
            self.down = links.send(plain(1, 2), self.one_down, **{axis: 3})
            self.last.append(links.send(plain(1, 1), self.two_up.at[1], **{axis: 1}))

    def middle(self):
        links, axis = self.links, self.axis
        self.up.wait_recv()
        self.mix_up[...] = (self.read(0, 1) + self.one_up[...].astype(F32)).astype(BF16)
        self.last.append(links.send(self.mix_up, self.two_up.at[0], **{axis: 1}))
        self.down.wait_recv()
        self.mix_down[...] = (self.read(1, 3) + self.one_down[...].astype(F32)).astype(BF16)
        self.last.append(links.send(self.mix_down, self.two_down.at[1], **{axis: 3}))

    def finish(self, store):
        for copy in self.last:
            copy.wait_recv()
        for half in range(2):
            store(
                half,
                self.read(half, 0)
                + self.two_up[half].astype(F32)
                + self.two_down[half].astype(F32),
            )


class Direct:
    def __init__(self, links, axis, read, plain, inbox):
        self.links, self.axis, self.read, self.plain, self.inbox = links, axis, read, plain, inbox

    def start(self):
        self.copies = [
            self.links.send(self.plain(step), self.inbox.at[step - 1], **{self.axis: step})
            for step in (1, 3, 2)
        ]

    def finish(self, store):
        for copy in self.copies:
            copy.wait_recv()
        for half in range(2):
            value = self.read(half)
            for index in range(3):
                value = value + self.inbox[index, half].astype(F32)
            store(half, value)


def dot(a, b):
    return jnp.dot(a, b, preferred_element_type=F32)


def dot_t(a, b):
    return lax.dot_general(a, b, (((1,), (1,)), ((), ())), preferred_element_type=F32)


def lanes_of(row, count):
    return jnp.transpose(jnp.broadcast_to(row[0:1], (128, count)))


def step_body(
    lat, noise, steps, layout, w_time, ws, wqk, wv, disc,
    grad_o, loss_o,
    send_sems, recv_sems, loc_sems,
    wt, wx_1, wx_2, ws_all, wx_1_all, wx_2_all, lat_all, mod, modin, mod_t, part, tin, mean_c, inv_c,
    tables, qk, q_t, probs, pv, vrow, logit_s, logit_r, dlog, d_sc, dv_t, dqk,
    stage, from_core, cross, from_chip, own, sums, stats_s, stats_r, dbr,
    loss_buf, loss_mid, z_send, z_recv, z_keep, *bufs,
):
    links = Links(send_sems, recv_sems)
    tokens, cols = noise.shape
    channels = lat.shape[1]
    rows_each = lat.shape[0]
    heads = cols // HD
    dp, zl, core = lax.axis_index("dp"), links.zl, links.core
    me = zl * 2 + core
    beside_me = zl * 2 + (core + 1) % 2
    far = ((zl + 1) % 2) * 2 + core
    far_beside = ((zl + 1) % 2) * 2 + (core + 1) % 2
    early = (heads - 1) // 2
    fold_at = early * 2 * HD
    late_at = fold_at + 128

    def col(owner, base=0):
        return pl.ds(pl.multiple_of(base + owner * cols, 128), cols)

    get_wt = pltpu.make_async_copy(w_time, wt, loc_sems.at[0])
    get_wt.start()
    links.barrier(NEAR)
    g_ws = Gather(links, ws, ws_all, loc_sems.at[1])
    g_1 = Gather(links, wx_1, wx_1_all, loc_sems.at[2])
    g_2 = Gather(links, wx_2, wx_2_all, loc_sems.at[4])
    g_ws.along_z()

    lane = lax.broadcasted_iota(jnp.int32, (ws.shape[0], 128), 1)
    scaled = wv[...].astype(F32) * disc[...].reshape(1, cols)
    extra = jnp.zeros((ws.shape[0], 128), F32)
    for head in range(heads):
        value = jnp.sum(scaled[:, head * HD : (head + 1) * HD], axis=1, keepdims=True)
        for term in range(3):
            piece = value.astype(BF16).astype(F32)
            extra = jnp.where(lane == term * 8 + head, piece, extra)
            value = value - piece
    wx_1[:, :fold_at] = wqk[:, :fold_at]
    wx_1[:, fold_at:] = extra.astype(BF16)
    wx_2[...] = wqk[:, fold_at:]
    g_1.along_z()
    own_lat = pltpu.make_async_copy(lat, lat_all.at[me], loc_sems.at[3])
    own_lat.start()
    halves = [slice(0, rows_each // 2), slice(rows_each // 2, rows_each)]
    across = [links.send(lat.at[h], lat_all.at[me, h], zl=1) for h in halves]
    beside = links.send(lat, lat_all.at[me], core=1)
    g_2.along_z()

    step_f = jnp.full((8, 128), steps[dp], jnp.int32).astype(F32)
    spot = lax.broadcasted_iota(jnp.int32, (8, 128), 1).astype(F32)
    angle = step_f * jnp.exp(-math.log(10000.0) * spot / (FREQ // 2))
    embed = jnp.concatenate([jnp.cos(angle), jnp.sin(angle)], axis=1).astype(BF16)
    sigma = (0.25 + 0.5 * step_f / STEPS)[0:1, 0:1]
    get_wt.wait()
    for third in range(3):
        here = slice(third * channels, (third + 1) * channels)
        mod[:, here] = dot(embed, wt[:, here])
    g_ws.spread(False)

    def norm_rows(owner):
        def rows16(index, carry):
            rows = pl.ds(pl.multiple_of(index * 16, 16), 16)
            value = lat_all[owner, rows].astype(F32)
            value = value - jnp.sum(value, axis=1, keepdims=True) * (1.0 / channels)
            spread = jnp.sum(value * value, axis=1, keepdims=True) * (1.0 / channels)
            value = value * lax.rsqrt(spread + ln_eps)
            value = value * (1.0 + mod[0:1, channels : 2 * channels]) + mod[0:1, :channels]
            modin[pl.ds(pl.multiple_of(owner * rows_each + index * 16, 16), 16)] = value.astype(BF16)
            return carry

        lax.fori_loop(0, rows_each // 16, rows16, 0)

    own_lat.wait()
    norm_rows(me)
    g_ws.relay()
    g_1.spread(False)
    beside.wait_recv()
    norm_rows(beside_me)
    g_ws.spread(True)
    g_1.relay()

    place_c = lanes_of(layout[...].astype(F32), tokens)
    lane = lax.broadcasted_iota(jnp.int32, (tokens, 128), 1)
    omega = jnp.exp(-math.log(10000.0) * (lane % 64).astype(F32) / 64)
    tables[0] = jnp.cos(place_c * omega)
    sine = jnp.sin(place_c * omega)
    tables[1] = jnp.where(lane < 64, -sine, sine)

    g_ws.relay()
    g_1.spread(True)
    passed = []
    for copy, h in zip(across, halves):
        copy.wait_recv()
        passed.append(links.send(lat_all.at[far, h], lat_all.at[far, h], core=1))
    norm_rows(far)
    g_2.spread(False)
    for copy in passed:
        copy.wait_recv()
    norm_rows(far_beside)

    def flip(index, carry):
        here = pl.ds(pl.multiple_of(index * 128, 128), 128)
        mod_t[here] = jnp.transpose(modin[:, here].astype(F32)).astype(BF16)
        return carry

    g_ws.settle()
    gate = mod[0:1, col(me, 2 * channels)]
    keep = 1.0 - sigma
    size = tokens // 2
    sent, near = [], []
    for index in range(2):
        rows = pl.ds(index * size, size)
        branch = dot(modin[rows], ws_all[...].reshape(channels, cols))
        mine = lat_all[pl.ds(index * 2, 2), :, col(me)].reshape(size, cols).astype(F32)
        mixed = keep * (mine + gate * branch) + sigma * noise[rows].astype(F32)
        part[rows] = mixed.astype(BF16)
        sent.append(links.send(part.at[rows], tin.at[rows, col(me)], zl=1))
        near.append(links.send(part.at[rows], tin.at[rows, col(me)], core=1))
        tin[rows, col(me)] = mixed.astype(BF16)
    g_1.relay()
    g_2.relay()
    g_2.spread(True)
    lax.fori_loop(0, channels // 128, flip, 0)

    passed = []
    for index in range(2):
        rows = pl.ds(index * size, size)
        sent[index].wait_recv()
        passed.append(links.send(tin.at[rows, col(far)], tin.at[rows, col(far)], core=1))
    tnorm_b = modin
    for index in range(2):
        near[index].wait_recv()
        passed[index].wait_recv()

        def rows16(step, carry):
            rows = pl.ds(pl.multiple_of(index * size + step * 16, 16), 16)
            value = tin[rows].astype(F32)
            mean = jnp.sum(value, axis=1, keepdims=True) * (1.0 / channels)
            value = value - mean
            spread = jnp.sum(value * value, axis=1, keepdims=True) * (1.0 / channels)
            inverse = lax.rsqrt(spread + ln_eps)
            tnorm_b[rows] = (value * inverse).astype(BF16)
            mean_c[rows] = jnp.broadcast_to(mean, (16, 128))
            inv_c[rows] = jnp.broadcast_to(inverse, (16, 128))
            return carry

        lax.fori_loop(0, size // 16, rows16, 0)
        if index == 0:
            g_2.relay()
    g_1.settle()

    def project(head, source, base):
        weights = source[:, :, :, :, pl.ds(pl.multiple_of(head * 256 - base, 256), 256)]
        both = dot(tnorm_b[...], weights.reshape(channels, 256))
        cosine, sine = tables[0], tables[1]
        query, key = both[:, :HD], both[:, HD:]
        query = query * cosine + pltpu.roll(query, 64, 1) * sine
        key = key * cosine + pltpu.roll(key, 64, 1) * sine
        qk[:, pl.ds(pl.multiple_of(head * 256, 256), 128)] = query.astype(BF16)
        qk[:, pl.ds(pl.multiple_of(head * 256 + 128, 128), 128)] = key.astype(BF16)
        q_t[head] = jnp.transpose(query).astype(BF16)

    scale_dot = 1.0 / math.sqrt(HD)
    block = 128
    blocks = tokens // block

    def attend(trip, carry):
        head, index = trip // blocks, trip % blocks
        rows = pl.ds(pl.multiple_of(index * block, block), block)
        query = qk[rows, pl.ds(pl.multiple_of(head * 256, 256), 128)]
        key = qk[:, pl.ds(pl.multiple_of(head * 256 + 128, 128), 128)]
        scores = dot_t(query, key) * scale_dot
        weights = jnp.exp(scores - jnp.max(scores, axis=1, keepdims=True))
        weights = weights * (1.0 / jnp.sum(weights, axis=1, keepdims=True))
        probs[head, rows] = weights
        share = jnp.sum(weights * vrow[pl.ds(head, 1)], axis=1, keepdims=True)
        pv[head, rows] = jnp.broadcast_to(share, (block, 128))
        return carry

    def project_early(head, carry):
        project(head, wx_1_all, 0)
        return carry

    def project_late(head, carry):
        project(head, wx_2_all, fold_at)
        return carry

    lax.fori_loop(0, early, project_early, 0)
    value_t = jnp.transpose(
        dot(tnorm_b[...], wx_1_all[:, :, :, :, pl.ds(fold_at, 128)].reshape(channels, 128))
    )
    vrow[...] = (value_t[0:8] + value_t[8:16] + value_t[16:24]).astype(BF16).astype(F32)
    lax.fori_loop(0, early * blocks, attend, 0)
    g_2.settle()
    links.drain()
    links.open = []
    lax.fori_loop(early, heads, project_late, 0)
    lax.fori_loop(early * blocks, heads * blocks, attend, 0)
    total = pv[0]
    for head in range(1, heads):
        total = total + pv[head]
    logit_s[...] = jnp.transpose(total)[0:8]
    tiny = [links.send(logit_s, logit_r.at[i], **step) for i, step in enumerate(CLIP_ALL)]
    dv_t[...] = jnp.zeros_like(dv_t)
    for copy in tiny:
        copy.wait_recv()
    logit = logit_s[...] + logit_r[0] + logit_r[1] + logit_r[2]
    soft = jnp.maximum(-logit, 0.0) + jnp.log1p(jnp.exp(-jnp.abs(logit)))
    loss = jnp.sum(soft, axis=1, keepdims=True) * (1.0 / tokens)
    lane = lax.broadcasted_iota(jnp.int32, (8, 128), 1)
    loss_mid[0] = jnp.where(lane == dp, jnp.broadcast_to(loss, (8, 128)), 0.0)

    def loss_step(index, axis):
        return [
            links.send(loss_mid.at[index], loss_buf.at[index, step - 1], **{axis: step})
            for step in (1, 2, 3)
        ]

    def loss_sum(index, copies):
        for copy in copies:
            copy.wait_recv()
        return loss_mid[index] + loss_buf[index, 0] + loss_buf[index, 1] + loss_buf[index, 2]

    tiny = loss_step(0, "y")
    dlog[...] = lanes_of((-1.0 / tokens) / (1.0 + jnp.exp(logit)), tokens)

    def backward(head, carry):
        def rows_of(index, d_value):
            rows = pl.ds(pl.multiple_of(index * block, block), block)
            weights = probs[head, rows]
            slope = dlog[rows][:, 0:1]
            tilt = vrow[pl.ds(head, 1)] - pv[head, rows][:, 0:1]
            d_sc[rows] = (weights * tilt * (slope * scale_dot)).astype(BF16)
            return d_value + jnp.sum(weights * slope, axis=0, keepdims=True)

        d_value = lax.fori_loop(0, blocks, rows_of, jnp.zeros((1, tokens), F32))
        d_value = d_value.astype(BF16).astype(F32)
        for term in range(3):
            dv_t[pl.ds(term * 8 + head, 1)] = d_value
        key = qk[:, pl.ds(pl.multiple_of(head * 256 + 128, 128), 128)]
        cosine, sine = tables[0], tables[1]
        d_query = dot(d_sc[...], key)
        d_key = jnp.transpose(dot(q_t[head], d_sc[...])).astype(BF16).astype(F32)
        d_query = d_query * cosine - pltpu.roll(d_query, 64, 1) * sine
        d_key = d_key * cosine - pltpu.roll(d_key, 64, 1) * sine
        start = head * 256 + ((head + early) // (2 * early)) * 128
        dqk[:, pl.ds(pl.multiple_of(start, 128), 128)] = d_query.astype(BF16)
        dqk[:, pl.ds(pl.multiple_of(start + 128, 128), 128)] = d_key.astype(BF16)
        return carry

    lax.fori_loop(0, heads, backward, 0)
    dqk[:, fold_at:late_at] = jnp.transpose(dv_t[...]).astype(BF16)
    loss_mid[1] = loss_sum(0, tiny)
    tiny = loss_step(1, "x")

    sums[...] = jnp.zeros_like(sums)

    def d_block(owner, rows):
        value = dot_t(dqk[rows, :late_at], wx_1_all[owner].reshape(cols, late_at))
        value = value + dot_t(dqk[rows, late_at:], wx_2_all[owner].reshape(cols, -1))
        normed = (tin[rows, col(owner)].astype(F32) - mean_c[rows][:, 0:1]) * inv_c[rows][:, 0:1]
        sums[0, rows] = sums[0, rows] + jnp.sum(value, axis=1, keepdims=True)
        sums[1, rows] = sums[1, rows] + jnp.sum(value * normed, axis=1, keepdims=True)
        return value

    pieces = [pl.ds(index * size, size) for index in range(2)]
    first, second, third = [], [], []
    for rows in pieces:
        stage[1, rows] = d_block(far_beside, rows).astype(BF16)
        first.append(links.send(stage.at[1, rows], from_core.at[1, rows], core=1))
    for index, rows in enumerate(pieces):
        value = d_block(far, rows)
        first[index].wait_recv()
        cross[rows] = (value + from_core[1, rows].astype(F32)).astype(BF16)
        second.append(links.send(cross.at[rows], from_chip.at[rows], zl=1))
    for rows in pieces:
        stage[0, rows] = d_block(beside_me, rows).astype(BF16)
        third.append(links.send(stage.at[0, rows], from_core.at[0, rows], core=1))
    for rows in pieces:
        own[rows] = d_block(me, rows)
    loss_mid[2] = loss_sum(1, tiny)
    tiny = loss_step(2, "zh")
    stats_s[0:8] = jnp.transpose(sums[0])[0:8]
    stats_s[8:16] = jnp.transpose(sums[1])[0:8]
    stats = [links.send(stats_s, stats_r.at[i], **step) for i, step in enumerate(CLIP_ALL)]
    for copy in stats:
        copy.wait_recv()
    both = (stats_s[...] + stats_r[0] + stats_r[1] + stats_r[2]) * (1.0 / channels)
    sums[0] = lanes_of(both[0:8], tokens)
    sums[1] = lanes_of(both[8:16], tokens)
    for index, rows in enumerate(pieces):
        third[index].wait_recv()
        second[index].wait_recv()
        value = own[rows] + from_core[0, rows].astype(F32) + from_chip[rows].astype(F32)
        inverse = inv_c[rows][:, 0:1]
        normed = (tin[rows, col(me)].astype(F32) - mean_c[rows][:, 0:1]) * inverse
        value = inverse * (value - sums[0, rows][:, 0:1] - normed * sums[1, rows][:, 0:1])
        dbr[rows] = (gate * keep * value).astype(BF16)

    grads = ws_all
    spare = list(bufs)
    stages = []
    for first_axis, second_axis, base in (("y", "x", 0), ("x", "y", 2)):
        big, spare = spare[:6], spare[6:]
        inbox, mid, mid_b = spare[:3]
        spare = spare[3:]

        def plain1(half, step, axis=first_axis, other=second_axis, base=base):
            return grads.at[slot_of(links, axis, step, other, base + half)]

        def read1(half, step, plain=plain1):
            return plain(half, step)[...].astype(F32)

        def spot_of(step, axis=second_axis):
            return ({"x": links.x, "y": links.y}[axis] + step) % 4

        def plain2(step, mid_b=mid_b, spot=spot_of):
            return mid_b.at[:, spot(step)]

        def read2(half, mid=mid, spot=spot_of):
            return mid[half, spot(0)]

        stages.append(
            (
                base,
                mid,
                mid_b,
                Scatter(links, first_axis, read1, plain1, big),
                Direct(links, second_axis, read2, plain2, inbox),
            )
        )
    for quarter in (0, 2, 1, 3):
        here = pl.ds(quarter * cols, cols)
        value = dot(mod_t[here], dbr[...]).astype(BF16)
        grads[quarter] = value.reshape(grads.shape[1:])
        stages[quarter // 2][3].start(quarter % 2)
    for pair in stages:
        pair[3].middle()
    for base, mid, mid_b, first_ring, second_ring in stages:

        def store(half, value, mid=mid, mid_b=mid_b):
            mid[half] = value
            mid_b[half] = value.astype(BF16)

        first_ring.finish(store)
        second_ring.start()
    for base, mid, mid_b, first_ring, second_ring in stages:

        def hold(half, value, base=base):
            z_keep[base + half] = value
            z_send[base + half] = value.astype(BF16)

        second_ring.finish(hold)
    tail = [
        links.send(z_send.at[(links.zh + step) % 4], z_recv.at[step - 1], zh=step)
        for step in (1, 3, 2)
    ]
    loss_o[...] = loss_sum(2, tiny)
    for copy in tail:
        copy.wait_recv()
    grad_o[...] = (
        z_keep[links.zh]
        + z_recv[0].astype(F32)
        + z_recv[1].astype(F32)
        + z_recv[2].astype(F32)
    )
    links.drain()


def shards(latents, noise, steps, layout, w_time, w_student, w_qk, w_value, w_disc):
    channels = latents.shape[1]
    tokens, cols = noise.shape
    rows = w_student.shape[0]
    heads = cols // HD
    wide = w_qk.shape[1] + 128
    narrow = (heads - 1) // 2 * 2 * HD + 128
    big = [VMEM((4, rows, cols), BF16)] * 4 + [VMEM((2, 4, rows, cols), BF16)] * 2
    small = [VMEM((3, 2, rows, cols), BF16)]
    mids = [VMEM((2, 4, rows, cols), F32), VMEM((2, 4, rows, cols), BF16)]
    scratch = [
        pltpu.SemaphoreType.DMA((160,)),
        pltpu.SemaphoreType.DMA((160,)),
        pltpu.SemaphoreType.DMA((5,)),
        VMEM(w_time.shape, BF16),
        VMEM((rows, narrow), BF16),
        VMEM((rows, wide - narrow), BF16),
        VMEM((4, 4, 4, rows, cols), BF16),
        VMEM((4, 4, 4, rows, narrow), BF16),
        VMEM((4, 4, 4, rows, wide - narrow), BF16),
        VMEM((4,) + latents.shape, BF16),
        VMEM((8, w_time.shape[1]), F32),
        VMEM((tokens, channels), BF16),
        VMEM((channels, tokens), BF16),
        VMEM((tokens, cols), BF16),
        VMEM((tokens, channels), BF16),
        VMEM((tokens, 128), F32),
        VMEM((tokens, 128), F32),
        VMEM((2, tokens, 128), F32),
        VMEM((tokens, 2 * cols), BF16),
        VMEM((heads, HD, tokens), BF16),
        VMEM((heads, tokens, tokens), F32),
        VMEM((heads, tokens, 128), F32),
        VMEM((8, tokens), F32),
        VMEM((8, tokens), F32),
        VMEM((3, 8, tokens), F32),
        VMEM((tokens, 128), F32),
        VMEM((tokens, tokens), BF16),
        VMEM((128, tokens), F32),
        VMEM((tokens, wide), BF16),
        VMEM((2, tokens, cols), BF16),
        VMEM((2, tokens, cols), BF16),
        VMEM((tokens, cols), BF16),
        VMEM((tokens, cols), BF16),
        VMEM((tokens, cols), F32),
        VMEM((2, tokens, 128), F32),
        VMEM((16, tokens), F32),
        VMEM((3, 16, tokens), F32),
        VMEM((tokens, cols), BF16),
        VMEM((3, 3, 8, 128), F32),
        VMEM((3, 8, 128), F32),
        VMEM((4, rows, cols), BF16),
        VMEM((3, rows, cols), BF16),
        VMEM((4, rows, cols), F32),
    ] + (big + small + mids) * 2
    student_grad, losses = pl.pallas_call(
        step_body,
        out_shape=(
            jax.ShapeDtypeStruct((rows, cols), F32),
            jax.ShapeDtypeStruct((8, 128), F32),
        ),
        in_specs=[
            VSPEC,
            VSPEC,
            pl.BlockSpec(memory_space=pltpu.SMEM),
            VSPEC,
            ASPEC,
            VSPEC,
            VSPEC,
            VSPEC,
            VSPEC,
        ],
        out_specs=(VSPEC, VSPEC),
        scratch_shapes=scratch,
        compiler_params=pltpu.CompilerParams(
            collective_id=1, has_side_effects=True, vmem_limit_bytes=67043328
        ),
    )(latents, noise, steps, layout, w_time, w_student, w_qk, w_value, w_disc)
    return (losses[0, : steps.shape[0]], student_grad)


def solution(mesh):
    return jax.shard_map(
        shards,
        mesh=mesh,
        in_specs=(
            P(("dp", "ctx"), None),
            P("dp", "ctx"),
            P(),
            P("dp", None),
            P(),
            P("dp", "ctx"),
            P("dp", "ctx"),
            P("dp", "ctx"),
            P("ctx"),
        ),
        out_specs=(P(), P("dp", "ctx")),
        check_vma=False,
    )
```

```python
import functools
import math

import jax
import jax.numpy as jnp
from jax import lax
from jax.experimental import pallas as pl
from jax.experimental.pallas import tpu as pltpu
from jax.sharding import PartitionSpec as P

HD = 128
FREQ = 256
STEPS = 1000
MESH = pl.DeviceIdType.MESH
VMEM = pltpu.VMEM
VSPEC = pl.BlockSpec(memory_space=pltpu.VMEM)
ASPEC = pl.BlockSpec(memory_space=pl.ANY)
F32 = jnp.float32
BF16 = jnp.bfloat16


ln_eps = 1e-06
exact_dots = lax.Precision.HIGHEST


def place():
    d = lax.axis_index("dp")
    c = lax.axis_index("ctx")
    return d // 16, (d // 4) % 4, d % 4, c // 2, c % 2


class Links:
    def __init__(self, send_sems, recv_sems):
        self.send_sems, self.recv_sems = send_sems, recv_sems
        self.used = 0
        self.open = []
        self.zh, self.x, self.y, self.zl, self.core = place()

    def dev(self, zh=0, x=0, y=0, zl=0, core=0):
        z_new = (self.zh + zh) % 4
        x_new = (self.x + x) % 4
        y_new = (self.y + y) % 4
        return (
            z_new * 16 + x_new * 4 + y_new,
            ((self.zl + zl) % 2) * 2 + (self.core + core) % 2,
        )

    def barrier(self, steps):
        sem = pltpu.get_barrier_semaphore()
        for step in steps:
            pl.semaphore_signal(sem, inc=1, device_id=self.dev(**step), device_id_type=MESH)
        pl.semaphore_wait(sem, len(steps))

    def send(self, src, dst, **step):
        slot = self.used
        self.used += 1
        copy = pltpu.make_async_remote_copy(
            src_ref=src,
            dst_ref=dst,
            send_sem=self.send_sems.at[slot],
            recv_sem=self.recv_sems.at[slot],
            device_id=self.dev(**step),
            device_id_type=MESH,
        )
        copy.start()
        self.open.append(copy)
        return copy

    def drain(self):
        for copy in self.open:
            copy.wait_send()


AXES_AB = (("x", "y", 0), ("y", "x", 2))


def slot_of(links, axis, step, other=None, zs=slice(0, 2)):
    moved = {"x": links.x, "y": links.y}
    moved[axis] = (moved[axis] + step) % 4
    picks = dict(moved)
    if other is not None:
        picks[other] = slice(None)
    return (zs, picks["x"], picks["y"])


class Gather:
    def __init__(self, links, shard, out, loc_sem):
        self.links, self.shard, self.out = links, shard, out
        self.own = pltpu.make_async_copy(shard, out.at[links.zh, links.x, links.y], loc_sem)

    def along_z(self):
        links = self.links
        self.own.start()
        home = self.out.at[links.zh, links.x, links.y]
        self.copies = [links.send(self.shard, home, zh=step) for step in (1, 3, 2)]

    def settle(self):
        for copy in self.copies:
            copy.wait_recv()
        self.copies = []

    def spread(self, second):
        links = self.links
        if not second:
            self.own.wait()
        self.settle()
        self.near = []
        for first_axis, second_axis, base in AXES_AB:
            axis = second_axis if second else first_axis
            other = first_axis if second else None
            half = [self.out.at[slot_of(links, axis, 0, other, base + i)] for i in range(2)]
            up = links.send(half[0], half[0], **{axis: 1})
            down = links.send(half[1], half[1], **{axis: 3})
            self.near.append((axis, other, base, up, down))
            self.copies.append(links.send(half[1], half[1], **{axis: 1}))
            self.copies.append(links.send(half[0], half[0], **{axis: 3}))

    def relay(self):
        links = self.links
        for axis, other, base, up, down in self.near:
            up.wait_recv()
            piece = self.out.at[slot_of(links, axis, 3, other, base)]
            self.copies.append(links.send(piece, piece, **{axis: 1}))
            down.wait_recv()
            piece = self.out.at[slot_of(links, axis, 1, other, base + 1)]
            self.copies.append(links.send(piece, piece, **{axis: 3}))


NEAR = (
    dict(core=1),
    dict(zl=1),
    dict(zl=1, core=1),
    dict(zh=1),
    dict(zh=2),
    dict(zh=3),
    dict(x=1),
    dict(x=2),
    dict(x=3),
    dict(y=1),
    dict(y=2),
    dict(y=3),
)
CLIP_ALL = NEAR[:3]


class Scatter:
    def __init__(self, links, axis, read, plain, bufs):
        self.links, self.axis, self.read, self.plain = links, axis, read, plain
        self.one_up, self.one_down, self.mix_up, self.mix_down, self.two_up, self.two_down = bufs
        self.last = []

    def start(self, half):
        links, axis, plain = self.links, self.axis, self.plain
        if half == 0:
            self.up = links.send(plain(0, 2), self.one_up, **{axis: 1})
            self.last.append(links.send(plain(0, 3), self.two_down.at[0], **{axis: 3}))
        else:
            self.down = links.send(plain(1, 2), self.one_down, **{axis: 3})
            self.last.append(links.send(plain(1, 1), self.two_up.at[1], **{axis: 1}))

    def middle(self):
        links, axis = self.links, self.axis
        self.up.wait_recv()
        self.mix_up[...] = (self.read(0, 1) + self.one_up[...].astype(F32)).astype(BF16)
        self.last.append(links.send(self.mix_up, self.two_up.at[0], **{axis: 1}))
        self.down.wait_recv()
        self.mix_down[...] = (self.read(1, 3) + self.one_down[...].astype(F32)).astype(BF16)
        self.last.append(links.send(self.mix_down, self.two_down.at[1], **{axis: 3}))

    def finish(self, store):
        for copy in self.last:
            copy.wait_recv()
        for half in range(2):
            store(
                half,
                self.read(half, 0)
                + self.two_up[half].astype(F32)
                + self.two_down[half].astype(F32),
            )


class Direct:
    def __init__(self, links, axis, read, plain, inbox):
        self.links, self.axis, self.read, self.plain, self.inbox = links, axis, read, plain, inbox

    def start(self):
        self.copies = [
            self.links.send(self.plain(step), self.inbox.at[step - 1], **{self.axis: step})
            for step in (1, 3, 2)
        ]

    def finish(self, store):
        for copy in self.copies:
            copy.wait_recv()
        for half in range(2):
            value = self.read(half)
            for index in range(3):
                value = value + self.inbox[index, half].astype(F32)
            store(half, value)


def dot(a, b):
    return jnp.dot(a, b, preferred_element_type=F32)


def dot_t(a, b):
    return lax.dot_general(a, b, (((1,), (1,)), ((), ())), preferred_element_type=F32)


def lanes_of(row, count):
    return jnp.transpose(jnp.broadcast_to(row[0:1], (128, count)))


def step_body(
    lat, noise, steps, layout, w_time, ws, wqk, wv, disc,
    grad_o, loss_o,
    send_sems, recv_sems, loc_sems,
    wt, wx_1, wx_2, ws_all, wx_1_all, wx_2_all, lat_all, mod, modin, mod_t, part, tin, mean_c, inv_c,
    tables, qk, q_t, probs, pv, vrow, logit_s, logit_r, dlog, d_sc, dv_t, dqk,
    stage, from_core, cross, from_chip, own, sums, stats_s, stats_r, dbr,
    loss_buf, loss_mid, z_send, z_recv, z_keep, *bufs,
):
    links = Links(send_sems, recv_sems)
    tokens, cols = noise.shape
    channels = lat.shape[1]
    rows_each = lat.shape[0]
    heads = cols // HD
    dp, zl, core = lax.axis_index("dp"), links.zl, links.core
    me = zl * 2 + core
    beside_me = zl * 2 + (core + 1) % 2
    far = ((zl + 1) % 2) * 2 + core
    far_beside = ((zl + 1) % 2) * 2 + (core + 1) % 2
    early = (heads - 1) // 2
    fold_at = early * 2 * HD
    late_at = fold_at + 128

    def col(owner, base=0):
        return pl.ds(pl.multiple_of(base + owner * cols, 128), cols)

    get_wt = pltpu.make_async_copy(w_time, wt, loc_sems.at[0])
    get_wt.start()
    links.barrier(NEAR)
    g_ws = Gather(links, ws, ws_all, loc_sems.at[1])
    g_1 = Gather(links, wx_1, wx_1_all, loc_sems.at[2])
    g_2 = Gather(links, wx_2, wx_2_all, loc_sems.at[4])
    g_ws.along_z()

    lane = lax.broadcasted_iota(jnp.int32, (ws.shape[0], 128), 1)
    scaled = wv[...].astype(F32) * disc[...].reshape(1, cols)
    extra = jnp.zeros((ws.shape[0], 128), F32)
    for head in range(heads):
        value = jnp.sum(scaled[:, head * HD : (head + 1) * HD], axis=1, keepdims=True)
        for term in range(3):
            piece = value.astype(BF16).astype(F32)
            extra = jnp.where(lane == term * 8 + head, piece, extra)
            value = value - piece
    wx_1[:, :fold_at] = wqk[:, :fold_at]
    wx_1[:, fold_at:] = extra.astype(BF16)
    wx_2[...] = wqk[:, fold_at:]
    g_1.along_z()
    own_lat = pltpu.make_async_copy(lat, lat_all.at[me], loc_sems.at[3])
    own_lat.start()
    halves = [slice(0, rows_each // 2), slice(rows_each // 2, rows_each)]
    across = [links.send(lat.at[h], lat_all.at[me, h], zl=1) for h in halves]
    beside = links.send(lat, lat_all.at[me], core=1)
    g_2.along_z()

    step_f = jnp.full((8, 128), steps[dp], jnp.int32).astype(F32)
    spot = lax.broadcasted_iota(jnp.int32, (8, 128), 1).astype(F32)
    angle = step_f * jnp.exp(-math.log(10000.0) * spot / (FREQ // 2))
    embed = jnp.concatenate([jnp.cos(angle), jnp.sin(angle)], axis=1).astype(BF16)
    sigma = (0.25 + 0.5 * step_f / STEPS)[0:1, 0:1]
    get_wt.wait()
    for third in range(3):
        here = slice(third * channels, (third + 1) * channels)
        mod[:, here] = dot(embed, wt[:, here])
    g_ws.spread(False)

    def norm_rows(owner):
        def rows16(index, carry):
            rows = pl.ds(pl.multiple_of(index * 16, 16), 16)
            value = lat_all[owner, rows].astype(F32)
            value = value - jnp.sum(value, axis=1, keepdims=True) * (1.0 / channels)
            spread = jnp.sum(value * value, axis=1, keepdims=True) * (1.0 / channels)
            value = value * lax.rsqrt(spread + ln_eps)
            value = value * (1.0 + mod[0:1, channels : 2 * channels]) + mod[0:1, :channels]
            modin[pl.ds(pl.multiple_of(owner * rows_each + index * 16, 16), 16)] = value.astype(BF16)
            return carry

        lax.fori_loop(0, rows_each // 16, rows16, 0)

    own_lat.wait()
    norm_rows(me)
    g_ws.relay()
    g_1.spread(False)
    beside.wait_recv()
    norm_rows(beside_me)
    g_ws.spread(True)
    g_1.relay()

    place_c = lanes_of(layout[...].astype(F32), tokens)
    lane = lax.broadcasted_iota(jnp.int32, (tokens, 128), 1)
    omega = jnp.exp(-math.log(10000.0) * (lane % 64).astype(F32) / 64)
    tables[0] = jnp.cos(place_c * omega)
    sine = jnp.sin(place_c * omega)
    tables[1] = jnp.where(lane < 64, -sine, sine)

    g_ws.relay()
    g_1.spread(True)
    passed = []
    for copy, h in zip(across, halves):
        copy.wait_recv()
        passed.append(links.send(lat_all.at[far, h], lat_all.at[far, h], core=1))
    norm_rows(far)
    g_2.spread(False)
    for copy in passed:
        copy.wait_recv()
    norm_rows(far_beside)

    def flip(index, carry):
        here = pl.ds(pl.multiple_of(index * 128, 128), 128)
        mod_t[here] = jnp.transpose(modin[:, here].astype(F32)).astype(BF16)
        return carry

    g_ws.settle()
    gate = mod[0:1, col(me, 2 * channels)]
    keep = 1.0 - sigma
    size = tokens // 2
    sent, near = [], []
    for index in range(2):
        rows = pl.ds(index * size, size)
        branch = dot(modin[rows], ws_all[...].reshape(channels, cols))
        mine = lat_all[pl.ds(index * 2, 2), :, col(me)].reshape(size, cols).astype(F32)
        mixed = keep * (mine + gate * branch) + sigma * noise[rows].astype(F32)
        part[rows] = mixed.astype(BF16)
        sent.append(links.send(part.at[rows], tin.at[rows, col(me)], zl=1))
        near.append(links.send(part.at[rows], tin.at[rows, col(me)], core=1))
        tin[rows, col(me)] = mixed.astype(BF16)
    g_1.relay()
    g_2.relay()
    g_2.spread(True)
    lax.fori_loop(0, channels // 128, flip, 0)

    passed = []
    for index in range(2):
        rows = pl.ds(index * size, size)
        sent[index].wait_recv()
        passed.append(links.send(tin.at[rows, col(far)], tin.at[rows, col(far)], core=1))
    tnorm_b = modin
    for index in range(2):
        near[index].wait_recv()
        passed[index].wait_recv()

        def rows16(step, carry):
            rows = pl.ds(pl.multiple_of(index * size + step * 16, 16), 16)
            value = tin[rows].astype(F32)
            mean = jnp.sum(value, axis=1, keepdims=True) * (1.0 / channels)
            value = value - mean
            spread = jnp.sum(value * value, axis=1, keepdims=True) * (1.0 / channels)
            inverse = lax.rsqrt(spread + ln_eps)
            tnorm_b[rows] = (value * inverse).astype(BF16)
            mean_c[rows] = jnp.broadcast_to(mean, (16, 128))
            inv_c[rows] = jnp.broadcast_to(inverse, (16, 128))
            return carry

        lax.fori_loop(0, size // 16, rows16, 0)
        if index == 0:
            g_2.relay()
    g_1.settle()

    def project(head, source, base):
        weights = source[:, :, :, :, pl.ds(pl.multiple_of(head * 256 - base, 256), 256)]
        both = dot(tnorm_b[...], weights.reshape(channels, 256))
        cosine, sine = tables[0], tables[1]
        query, key = both[:, :HD], both[:, HD:]
        query = query * cosine + pltpu.roll(query, 64, 1) * sine
        key = key * cosine + pltpu.roll(key, 64, 1) * sine
        qk[:, pl.ds(pl.multiple_of(head * 256, 256), 128)] = query.astype(BF16)
        qk[:, pl.ds(pl.multiple_of(head * 256 + 128, 128), 128)] = key.astype(BF16)
        q_t[head] = jnp.transpose(query).astype(BF16)

    scale_dot = 1.0 / math.sqrt(HD)
    block = 128
    blocks = tokens // block

    def attend(trip, carry):
        head, index = trip // blocks, trip % blocks
        rows = pl.ds(pl.multiple_of(index * block, block), block)
        query = qk[rows, pl.ds(pl.multiple_of(head * 256, 256), 128)]
        key = qk[:, pl.ds(pl.multiple_of(head * 256 + 128, 128), 128)]
        scores = dot_t(query, key) * scale_dot
        weights = jnp.exp(scores - jnp.max(scores, axis=1, keepdims=True))
        weights = weights * (1.0 / jnp.sum(weights, axis=1, keepdims=True))
        probs[head, rows] = weights
        share = jnp.sum(weights * vrow[pl.ds(head, 1)], axis=1, keepdims=True)
        pv[head, rows] = jnp.broadcast_to(share, (block, 128))
        return carry

    def project_early(head, carry):
        project(head, wx_1_all, 0)
        return carry

    def project_late(head, carry):
        project(head, wx_2_all, fold_at)
        return carry

    lax.fori_loop(0, early, project_early, 0)
    value_t = jnp.transpose(
        dot(tnorm_b[...], wx_1_all[:, :, :, :, pl.ds(fold_at, 128)].reshape(channels, 128))
    )
    vrow[...] = (value_t[0:8] + value_t[8:16] + value_t[16:24]).astype(BF16).astype(F32)
    lax.fori_loop(0, early * blocks, attend, 0)
    g_2.settle()
    links.drain()
    links.open = []
    lax.fori_loop(early, heads, project_late, 0)
    lax.fori_loop(early * blocks, heads * blocks, attend, 0)
    total = pv[0]
    for head in range(1, heads):
        total = total + pv[head]
    logit_s[...] = jnp.transpose(total)[0:8]
    tiny = [links.send(logit_s, logit_r.at[i], **step) for i, step in enumerate(CLIP_ALL)]
    dv_t[...] = jnp.zeros_like(dv_t)
    for copy in tiny:
        copy.wait_recv()
    logit = logit_s[...] + logit_r[0] + logit_r[1] + logit_r[2]
    soft = jnp.maximum(-logit, 0.0) + jnp.log1p(jnp.exp(-jnp.abs(logit)))
    loss = jnp.sum(soft, axis=1, keepdims=True) * (1.0 / tokens)
    lane = lax.broadcasted_iota(jnp.int32, (8, 128), 1)
    loss_mid[0] = jnp.where(lane == dp, jnp.broadcast_to(loss, (8, 128)), 0.0)

    def loss_step(index, axis):
        return [
            links.send(loss_mid.at[index], loss_buf.at[index, step - 1], **{axis: step})
            for step in (1, 2, 3)
        ]

    def loss_sum(index, copies):
        for copy in copies:
            copy.wait_recv()
        return loss_mid[index] + loss_buf[index, 0] + loss_buf[index, 1] + loss_buf[index, 2]

    tiny = loss_step(0, "y")
    dlog[...] = lanes_of((-1.0 / tokens) / (1.0 + jnp.exp(logit)), tokens)

    def backward(head, carry):
        def rows_of(index, d_value):
            rows = pl.ds(pl.multiple_of(index * block, block), block)
            weights = probs[head, rows]
            slope = dlog[rows][:, 0:1]
            tilt = vrow[pl.ds(head, 1)] - pv[head, rows][:, 0:1]
            d_sc[rows] = (weights * tilt * (slope * scale_dot)).astype(BF16)
            return d_value + jnp.sum(weights * slope, axis=0, keepdims=True)

        d_value = lax.fori_loop(0, blocks, rows_of, jnp.zeros((1, tokens), F32))
        d_value = d_value.astype(BF16).astype(F32)
        for term in range(3):
            dv_t[pl.ds(term * 8 + head, 1)] = d_value
        key = qk[:, pl.ds(pl.multiple_of(head * 256 + 128, 128), 128)]
        cosine, sine = tables[0], tables[1]
        d_query = dot(d_sc[...], key)
        d_key = jnp.transpose(dot(q_t[head], d_sc[...])).astype(BF16).astype(F32)
        d_query = d_query * cosine - pltpu.roll(d_query, 64, 1) * sine
        d_key = d_key * cosine - pltpu.roll(d_key, 64, 1) * sine
        start = head * 256 + ((head + early) // (2 * early)) * 128
        dqk[:, pl.ds(pl.multiple_of(start, 128), 128)] = d_query.astype(BF16)
        dqk[:, pl.ds(pl.multiple_of(start + 128, 128), 128)] = d_key.astype(BF16)
        return carry

    lax.fori_loop(0, heads, backward, 0)
    dqk[:, fold_at:late_at] = jnp.transpose(dv_t[...]).astype(BF16)
    loss_mid[1] = loss_sum(0, tiny)
    tiny = loss_step(1, "x")

    sums[...] = jnp.zeros_like(sums)

    def d_block(owner, rows):
        value = dot_t(dqk[rows, :late_at], wx_1_all[owner].reshape(cols, late_at))
        value = value + dot_t(dqk[rows, late_at:], wx_2_all[owner].reshape(cols, -1))
        normed = (tin[rows, col(owner)].astype(F32) - mean_c[rows][:, 0:1]) * inv_c[rows][:, 0:1]
        sums[0, rows] = sums[0, rows] + jnp.sum(value, axis=1, keepdims=True)
        sums[1, rows] = sums[1, rows] + jnp.sum(value * normed, axis=1, keepdims=True)
        return value

    pieces = [pl.ds(index * size, size) for index in range(2)]
    first, second, third = [], [], []
    for index, rows in enumerate(pieces):
        stage[1, rows] = d_block(far_beside, rows).astype(BF16)
        first.append(links.send(stage.at[1, rows], from_core.at[1, rows], core=1))
        value = d_block(far, rows)
        first[index].wait_recv()
        cross[rows] = (value + from_core[1, rows].astype(F32)).astype(BF16)
        second.append(links.send(cross.at[rows], from_chip.at[rows], zl=1))
    for rows in pieces:
        stage[0, rows] = d_block(beside_me, rows).astype(BF16)
        third.append(links.send(stage.at[0, rows], from_core.at[0, rows], core=1))
    for rows in pieces:
        own[rows] = d_block(me, rows)
    loss_mid[2] = loss_sum(1, tiny)
    tiny = loss_step(2, "zh")
    stats_s[0:8] = jnp.transpose(sums[0])[0:8]
    stats_s[8:16] = jnp.transpose(sums[1])[0:8]
    stats = [links.send(stats_s, stats_r.at[i], **step) for i, step in enumerate(CLIP_ALL)]
    for copy in stats:
        copy.wait_recv()
    both = (stats_s[...] + stats_r[0] + stats_r[1] + stats_r[2]) * (1.0 / channels)
    sums[0] = lanes_of(both[0:8], tokens)
    sums[1] = lanes_of(both[8:16], tokens)
    for index, rows in enumerate(pieces):
        third[index].wait_recv()
        second[index].wait_recv()
        value = own[rows] + from_core[0, rows].astype(F32) + from_chip[rows].astype(F32)
        inverse = inv_c[rows][:, 0:1]
        normed = (tin[rows, col(me)].astype(F32) - mean_c[rows][:, 0:1]) * inverse
        value = inverse * (value - sums[0, rows][:, 0:1] - normed * sums[1, rows][:, 0:1])
        dbr[rows] = (gate * keep * value).astype(BF16)

    grads = ws_all
    spare = list(bufs)
    stages = []
    for first_axis, second_axis, base in (("y", "x", 0), ("x", "y", 2)):
        big, spare = spare[:6], spare[6:]
        inbox, mid, mid_b = spare[:3]
        spare = spare[3:]

        def plain1(half, step, axis=first_axis, other=second_axis, base=base):
            return grads.at[slot_of(links, axis, step, other, base + half)]

        def read1(half, step, plain=plain1):
            return plain(half, step)[...].astype(F32)

        def spot_of(step, axis=second_axis):
            return ({"x": links.x, "y": links.y}[axis] + step) % 4

        def plain2(step, mid_b=mid_b, spot=spot_of):
            return mid_b.at[:, spot(step)]

        def read2(half, mid=mid, spot=spot_of):
            return mid[half, spot(0)]

        stages.append(
            (
                base,
                mid,
                mid_b,
                Scatter(links, first_axis, read1, plain1, big),
                Direct(links, second_axis, read2, plain2, inbox),
            )
        )
    for quarter in (0, 2, 1, 3):
        here = pl.ds(quarter * cols, cols)
        value = dot(mod_t[here], dbr[...]).astype(BF16)
        grads[quarter] = value.reshape(grads.shape[1:])
        stages[quarter // 2][3].start(quarter % 2)
    for pair in stages:
        pair[3].middle()
    for base, mid, mid_b, first_ring, second_ring in stages:

        def store(half, value, mid=mid, mid_b=mid_b):
            mid[half] = value
            mid_b[half] = value.astype(BF16)

        first_ring.finish(store)
        second_ring.start()
    for base, mid, mid_b, first_ring, second_ring in stages:

        def hold(half, value, base=base):
            z_keep[base + half] = value
            z_send[base + half] = value.astype(BF16)

        second_ring.finish(hold)
    tail = [
        links.send(z_send.at[(links.zh + step) % 4], z_recv.at[step - 1], zh=step)
        for step in (1, 3, 2)
    ]
    loss_o[...] = loss_sum(2, tiny)
    for copy in tail:
        copy.wait_recv()
    grad_o[...] = (
        z_keep[links.zh]
        + z_recv[0].astype(F32)
        + z_recv[1].astype(F32)
        + z_recv[2].astype(F32)
    )
    links.drain()


def shards(latents, noise, steps, layout, w_time, w_student, w_qk, w_value, w_disc):
    channels = latents.shape[1]
    tokens, cols = noise.shape
    rows = w_student.shape[0]
    heads = cols // HD
    wide = w_qk.shape[1] + 128
    narrow = (heads - 1) // 2 * 2 * HD + 128
    big = [VMEM((4, rows, cols), BF16)] * 4 + [VMEM((2, 4, rows, cols), BF16)] * 2
    small = [VMEM((3, 2, rows, cols), BF16)]
    mids = [VMEM((2, 4, rows, cols), F32), VMEM((2, 4, rows, cols), BF16)]
    scratch = [
        pltpu.SemaphoreType.DMA((160,)),
        pltpu.SemaphoreType.DMA((160,)),
        pltpu.SemaphoreType.DMA((5,)),
        VMEM(w_time.shape, BF16),
        VMEM((rows, narrow), BF16),
        VMEM((rows, wide - narrow), BF16),
        VMEM((4, 4, 4, rows, cols), BF16),
        VMEM((4, 4, 4, rows, narrow), BF16),
        VMEM((4, 4, 4, rows, wide - narrow), BF16),
        VMEM((4,) + latents.shape, BF16),
        VMEM((8, w_time.shape[1]), F32),
        VMEM((tokens, channels), BF16),
        VMEM((channels, tokens), BF16),
        VMEM((tokens, cols), BF16),
        VMEM((tokens, channels), BF16),
        VMEM((tokens, 128), F32),
        VMEM((tokens, 128), F32),
        VMEM((2, tokens, 128), F32),
        VMEM((tokens, 2 * cols), BF16),
        VMEM((heads, HD, tokens), BF16),
        VMEM((heads, tokens, tokens), F32),
        VMEM((heads, tokens, 128), F32),
        VMEM((8, tokens), F32),
        VMEM((8, tokens), F32),
        VMEM((3, 8, tokens), F32),
        VMEM((tokens, 128), F32),
        VMEM((tokens, tokens), BF16),
        VMEM((128, tokens), F32),
        VMEM((tokens, wide), BF16),
        VMEM((2, tokens, cols), BF16),
        VMEM((2, tokens, cols), BF16),
        VMEM((tokens, cols), BF16),
        VMEM((tokens, cols), BF16),
        VMEM((tokens, cols), F32),
        VMEM((2, tokens, 128), F32),
        VMEM((16, tokens), F32),
        VMEM((3, 16, tokens), F32),
        VMEM((tokens, cols), BF16),
        VMEM((3, 3, 8, 128), F32),
        VMEM((3, 8, 128), F32),
        VMEM((4, rows, cols), BF16),
        VMEM((3, rows, cols), BF16),
        VMEM((4, rows, cols), F32),
    ] + (big + small + mids) * 2
    student_grad, losses = pl.pallas_call(
        step_body,
        out_shape=(
            jax.ShapeDtypeStruct((rows, cols), F32),
            jax.ShapeDtypeStruct((8, 128), F32),
        ),
        in_specs=[
            VSPEC,
            VSPEC,
            pl.BlockSpec(memory_space=pltpu.SMEM),
            VSPEC,
            ASPEC,
            VSPEC,
            VSPEC,
            VSPEC,
            VSPEC,
        ],
        out_specs=(VSPEC, VSPEC),
        scratch_shapes=scratch,
        compiler_params=pltpu.CompilerParams(
            collective_id=1, has_side_effects=True, vmem_limit_bytes=67043328
        ),
    )(latents, noise, steps, layout, w_time, w_student, w_qk, w_value, w_disc)
    return (losses[0, : steps.shape[0]], student_grad)


def solution(mesh):
    return jax.shard_map(
        shards,
        mesh=mesh,
        in_specs=(
            P(("dp", "ctx"), None),
            P("dp", "ctx"),
            P(),
            P("dp", None),
            P(),
            P("dp", "ctx"),
            P("dp", "ctx"),
            P("dp", "ctx"),
            P("ctx"),
        ),
        out_specs=(P(), P("dp", "ctx")),
        check_vma=False,
    )
```
